128 devices in a mesh: dp: 16 (over z, x), mp: 8 (over y, core).
Axes of the slice: x: 4, y: 4, z: 4, core: 2. Of those that a mesh axis runs over, the one named last changes fastest.
Arguments:
- tokens: bfloat16 [6144, 8192], P('dp', 'mp'), may hold values from -6 to 6
- cotangent: bfloat16 [6144, 8192], P('dp', 'mp'), may hold values from -6 to 6
- seq_right: bfloat16 [48, 128, 128], P('dp'), may hold values from -0.5 to 0.5
- seq_left: bfloat16 [128, 48, 48], P('dp'), may hold values from -0.875 to 0.875
- seq_gain: float32 [8192], P('mp'), may hold values from 0.5 to 2
- right_one: bfloat16 [64, 512, 128], P('mp'), may hold values from -0.5 to 0.5
- left_one: bfloat16 [512, 64, 64], P('mp'), may hold values from -0.75 to 0.75
- left_two: bfloat16 [512, 64, 64], P('mp'), may hold values from -0.75 to 0.75
- right_two: bfloat16 [64, 128, 512], P('mp'), may hold values from -0.25 to 0.25
Outputs:
- output: bfloat16 [6144, 8192], P('dp', 'mp')
- grad_tokens: bfloat16 [6144, 8192], P('dp', 'mp')
- grad_seq_right: float32 [48, 128, 128], P('dp')
- grad_seq_left: float32 [128, 48, 48], P('dp')
- grad_gain: float32 [8192], P('mp')
- grad_right_one: float32 [64, 512, 128], P('mp')
- grad_left_one: float32 [512, 64, 64], P('mp')
- grad_left_two: float32 [512, 64, 64], P('mp')
- grad_right_two: float32 [64, 128, 512], P('mp')
The draws below stay inside these ranges and needn't reach their ends.
All inputs are finite; a program needn't handle non-finite values.
Results may differ from the reference program's by a relative error of at most 0.01.
Values may be sent and summed in bfloat16 or wider, within the bound.
No kernel may reach another device: no remote copies, remote signals or barrier semaphores. Data moves between devices by JAX's collectives and lax.ppermute only.
A program may use at most 128 MiB of HBM per device.

```python
import math
import jax
import jax.numpy as jnp
from jax import lax

B1 = 64
BS = 128
SB = 128
TOK_DEV = 384
D = 8192
HB = 512
SEQ = 6144
S1 = 48
N_DP = 16


def block_levels(key, shape, split, least, high):
    gain = 1.0
    for dim, shards_of in split:
        steps = jax.random.uniform(jax.random.fold_in(jax.random.fold_in(key, 6), dim), (shards_of,), jnp.float32, least / len(split), high / len(split))
        gain = gain * jnp.repeat(jnp.exp(steps), shape[dim] // shards_of).reshape((-1,) + (1,) * (len(shape) - 1 - dim))
    return gain


def bell_draw(rng, shape, width, most, cuts=(), kind=jnp.bfloat16):
    level = block_levels(rng, shape, cuts, -0.22, 0.18) if cuts else 1.0
    drawn = jax.random.normal(rng, shape, jnp.float32) * width * level
    return jnp.minimum(jnp.maximum(drawn, -most), most).astype(kind)


def setup_inputs(seed: int = 0) -> dict:
    keys = jax.random.split(jax.random.key(seed), 10)
    tokens = bell_draw(keys[0], (SEQ, D), 1.0, 6.0, ((0, 16), (1, 8)))
    cotangent = bell_draw(keys[1], (SEQ, D), 1.0, 6.0, ((0, 16), (1, 8)))
    seq_right = bell_draw(keys[2], (S1, SB, SB), SB ** -0.5, 0.5, ((0, 16),))
    seq_left = bell_draw(keys[3], (SB, S1, S1), S1 ** -0.5, 0.875, ((0, 16),))
    seq_gain = jnp.clip(jnp.exp(math.log(2.0) - 1.3862944 * jax.random.uniform(keys[4], (D,), jnp.float32) ** block_levels(keys[4], (D,), ((0, 8),), -0.2, 0.2)), 0.5, 2.0)
    right_one = bell_draw(keys[5], (B1, HB, BS), BS ** -0.5, 0.5, ((0, 8),))
    left_one = bell_draw(keys[6], (HB, B1, B1), B1 ** -0.5, 0.75, ((0, 8),))
    left_two = bell_draw(keys[7], (HB, B1, B1), B1 ** -0.5, 0.75, ((0, 8),))
    right_two = bell_draw(keys[8], (B1, BS, HB), HB ** -0.5, 0.25, ((0, 8),))
    return dict(tokens=tokens, cotangent=cotangent, seq_right=seq_right, seq_left=seq_left, seq_gain=seq_gain, right_one=right_one, left_one=left_one, left_two=left_two, right_two=right_two)


def as_float(value):
    return value.astype(jnp.float32)

def gelu_value(value):
    return value * 0.5 * (1.0 + jax.scipy.special.erf(value / math.sqrt(2.0)))

def gelu_slope(value):
    cdf_part = 0.5 * (1.0 + jax.scipy.special.erf(value / math.sqrt(2.0)))
    return cdf_part + value * jnp.exp(-0.5 * value * value) / math.sqrt(2.0 * math.pi)

def reference(tokens, cotangent, seq_right, seq_left, seq_gain, right_one, left_one, left_two, right_two):
    seq_view = tokens.reshape(S1, SB, D)
    first = jnp.einsum('sij,sjc->sic', as_float(seq_right), as_float(seq_view)).astype(jnp.bfloat16)
    mixed = jnp.einsum('isk,kic->sic', as_float(seq_left), as_float(first)).astype(jnp.bfloat16)
    blend = (as_float(seq_view) + seq_gain * as_float(mixed)).astype(jnp.bfloat16)
    blend_blocks = blend.reshape(N_DP, TOK_DEV, B1, BS)
    grad_blocks = cotangent.reshape(N_DP, TOK_DEV, B1, BS)

    def feature_block(carry, inputs):
        zview, gview = inputs
        act_a = jnp.einsum('bij,tbj->tbi', as_float(right_one), as_float(zview)).astype(jnp.bfloat16)
        pre = jnp.einsum('ibk,tki->tbi', as_float(left_one), as_float(act_a))
        hidden = gelu_value(pre).astype(jnp.bfloat16)
        act_c = jnp.einsum('ibk,tki->tbi', as_float(left_two), as_float(hidden)).astype(jnp.bfloat16)
        last = jnp.einsum('bij,tbj->tbi', as_float(right_two), as_float(act_c))
        result = (as_float(zview) + last).astype(jnp.bfloat16)
        back_c = jnp.einsum('bij,tbi->tbj', as_float(right_two), as_float(gview)).astype(jnp.bfloat16)
        sum_r2 = jnp.einsum('tbi,tbj->bij', as_float(gview), as_float(act_c))
        back_h = jnp.einsum('ibk,tbi->tki', as_float(left_two), as_float(back_c))
        back_pre = (back_h * gelu_slope(pre)).astype(jnp.bfloat16)
        sum_l2 = jnp.einsum('tbi,tki->ibk', as_float(back_c), as_float(hidden))
        back_a = jnp.einsum('ibk,tbi->tki', as_float(left_one), as_float(back_pre)).astype(jnp.bfloat16)
        sum_l1 = jnp.einsum('tbi,tki->ibk', as_float(back_pre), as_float(act_a))
        back_zz = jnp.einsum('bij,tbi->tbj', as_float(right_one), as_float(back_a))
        sum_r1 = jnp.einsum('tbi,tbj->bij', as_float(back_a), as_float(zview))
        back_z = as_float(gview) + back_zz
        totals = (carry[0] + sum_r1, carry[1] + sum_l1, carry[2] + sum_l2, carry[3] + sum_r2)
        return (totals, (result, back_z))
    start = (jnp.zeros((B1, HB, BS), jnp.float32), jnp.zeros((HB, B1, B1), jnp.float32), jnp.zeros((HB, B1, B1), jnp.float32), jnp.zeros((B1, BS, HB), jnp.float32))
    totals, outs = lax.scan(feature_block, start, (blend_blocks, grad_blocks))
    output = outs[0].reshape(SEQ, D)
    back_z = outs[1].reshape(S1, SB, D)
    scale_rows = float(SEQ) ** (-0.5)
    scale_cols = float(D) ** (-0.5)
    grad_gain = lax.optimization_barrier(jnp.sum(back_z * as_float(mixed), axis=(0, 1))) * scale_rows
    back_mixed = (back_z * seq_gain).astype(jnp.bfloat16)
    back_first = jnp.einsum('isk,sic->kic', as_float(seq_left), as_float(back_mixed)).astype(jnp.bfloat16)
    grad_seq_left = jnp.einsum('sic,kic->isk', as_float(back_mixed), as_float(first)) * scale_cols
    grad_tokens = (back_z + jnp.einsum('sij,sic->sjc', as_float(seq_right), as_float(back_first))).astype(jnp.bfloat16)
    grad_seq_right = jnp.einsum('sic,sjc->sij', as_float(back_first), as_float(seq_view)) * scale_cols
    return (output, grad_tokens.reshape(SEQ, D), grad_seq_right, grad_seq_left, grad_gain, totals[0] * scale_rows, totals[1] * scale_rows, totals[2] * scale_rows, totals[3] * scale_rows)
```

```python
import math

import jax
import jax.numpy as jnp
from jax import lax
from jax.experimental import pallas as pl
from jax.experimental.pallas import tpu as pltpu
from jax.sharding import PartitionSpec as P

BF = jnp.bfloat16
F32 = jnp.float32
VMEM_BYTES = 56 * 1024 * 1024


def dot(left_arg, right_arg, left_dim, right_dim):
    return lax.dot_general(
        left_arg,
        right_arg,
        (((left_dim,), (right_dim,)), ((), ())),
        preferred_element_type=F32,
    )


def product(form, left_arg, right_arg):
    return jnp.einsum(form, left_arg, right_arg, preferred_element_type=F32)


def sum_slice(parts):
    n = lax.axis_size("dp")
    mine = lax.all_to_all(parts.reshape(n, -1, parts.shape[-1]), "dp", split_axis=0, concat_axis=0, tiled=True)
    return jnp.sum(mine.astype(F32), axis=0)


def all_slices(piece):
    n = lax.axis_size("dp")
    copies = jnp.broadcast_to(piece[None], (n,) + piece.shape)
    return lax.all_to_all(copies, "dp", split_axis=0, concat_axis=0, tiled=True)


def sum_over_mp(value):
    n = lax.axis_size("mp")
    core = lax.axis_index("mp") % 2
    half = value.shape[0] // 2
    halves = value.reshape(2, half, value.shape[1])
    mine = lax.dynamic_index_in_dim(halves, core, 0, keepdims=False)
    other = lax.dynamic_index_in_dim(halves, 1 - core, 0, keepdims=False)
    swap = [(i, i ^ 1) for i in range(n)]
    mine = mine + lax.ppermute(other, "mp", swap)
    total = mine
    for d in range(2, n, 2):
        total = total + lax.ppermute(mine, "mp", [(i, i ^ d) for i in range(n)])
    other = lax.ppermute(total, "mp", swap)
    return jnp.where(core == 0, jnp.concatenate([total, other]), jnp.concatenate([other, total]))


def params():
    return pltpu.CompilerParams(vmem_limit_bytes=VMEM_BYTES)


def expand(x, weight, parts, me):
    blocks, hidden, feats = weight.shape
    tokens = x.shape[0]
    lanes = tokens // 128
    rows = hidden // parts * blocks

    def body(me_ref, x_ref, w_ref, *refs):
        outs, wide_ref = refs[:parts], refs[parts]
        for b in range(blocks):
            part = dot(w_ref[b], x_ref[:, b * feats : (b + 1) * feats], 1, 1)
            for c in range(lanes):
                wide_ref[c, pl.ds(b, hidden, stride=blocks), :] = part[:, c * 128 : (c + 1) * 128]
        for d in range(parts):
            start = pl.multiple_of((me_ref[0] ^ d) * rows, rows)
            for c in range(lanes):
                outs[d][:, c * 128 : (c + 1) * 128] = wide_ref[c, pl.ds(start, rows), :].astype(BF)

    return pl.pallas_call(
        body,
        in_specs=[pl.BlockSpec(memory_space=pltpu.SMEM)] + [pl.BlockSpec(memory_space=pltpu.VMEM)] * 2,
        out_specs=[pl.BlockSpec(memory_space=pltpu.VMEM)] * parts,
        out_shape=[jax.ShapeDtypeStruct((rows, tokens), BF)] * parts,
        scratch_shapes=[pltpu.VMEM((lanes, hidden * blocks, 128), F32)],
        compiler_params=params(),
        name="expand",
    )(me, x, weight)


def send(pieces, *which):
    n = len(pieces)
    return {d: lax.ppermute(pieces[d], "mp", [(i, i ^ d) for i in range(n)]) for d in which}


def together(*values):
    return lax.optimization_barrier(values)


def in_order(pieces, *groups):
    got = {0: pieces[0]}
    for group in groups:
        got.update(group)
    return [got[d] for d in range(len(pieces))]


STEP = 8


def gather_pair(refs, pair, me_ref, mix_ref):
    for d, ref in enumerate(refs):
        wide = ref[pair * 16 : pair * 16 + 16, :].astype(F32)
        at = pl.multiple_of((me_ref[0] ^ d) * 8, 8)
        for h in range(2):
            mix_ref[h, pl.ds(at, 8), :] = wide[h * 8 : h * 8 + 8]
    return [mix_ref[h].astype(BF) for h in range(2)]


def spread_pair(values, refs, pair, me_ref, mix_ref):
    for h in range(2):
        mix_ref[h] = values[h]
    for d, ref in enumerate(refs):
        at = pl.multiple_of((me_ref[0] ^ d) * 8, 8)
        block = jnp.concatenate([mix_ref[h, pl.ds(at, 8), :] for h in range(2)], axis=0)
        ref[pair * 16 : pair * 16 + 16, :] = block.astype(BF)


def middle_main(act, back, left_one, left_one_t, left_two_t, me):
    n = len(act)
    tokens = act[0].shape[1]
    units, width, _ = left_one.shape

    def body(me_ref, *refs):
        acts, backs, (one_ref, one_t_ref, two_t_ref) = refs[:n], refs[n : 2 * n], refs[2 * n : 2 * n + 3]
        outs = refs[2 * n + 3 : 3 * n + 3]
        x_ref, c_ref, hid_ref, bp_ref, mix_a, mix_c, mix_o = refs[3 * n + 3 :]
        for pair in range(STEP // 2):
            xs = gather_pair(acts, pair, me_ref, mix_a)
            cs = gather_pair(backs, pair, me_ref, mix_c)
            values = []
            for h in range(2):
                i = pair * 2 + h
                pre = dot(one_ref[i], xs[h], 1, 0)
                back_h = dot(two_t_ref[i], cs[h], 1, 0)
                cdf = 0.5 * (1.0 + lax.erf(pre * (1.0 / math.sqrt(2.0))))
                slope = cdf + pre * jnp.exp(-0.5 * pre * pre) * (1.0 / math.sqrt(2.0 * math.pi))
                back_pre = (back_h * slope).astype(BF)
                x_ref[i] = xs[h]
                c_ref[i] = cs[h]
                hid_ref[i] = (pre * cdf).astype(BF)
                bp_ref[i] = back_pre
                values.append(dot(one_t_ref[i], back_pre, 1, 0))
            spread_pair(values, outs, pair, me_ref, mix_o)

    piece = pl.BlockSpec((STEP * 8, tokens), lambda g: (g, 0))
    weights = pl.BlockSpec((STEP, width, width), lambda g: (g, 0, 0))
    local = pl.BlockSpec((STEP, width, tokens), lambda g: (g, 0, 0))
    results = pl.pallas_call(
        body,
        grid=(units // STEP,),
        in_specs=[pl.BlockSpec(memory_space=pltpu.SMEM)] + [piece] * (2 * n) + [weights] * 3,
        out_specs=[piece] * n + [local] * 4,
        out_shape=[jax.ShapeDtypeStruct(act[0].shape, BF)] * n
        + [jax.ShapeDtypeStruct((units, width, tokens), BF)] * 4,
        scratch_shapes=[pltpu.VMEM((2, width, tokens), F32)] * 3,
        compiler_params=params(),
        name="middle_main",
    )(me, *act, *back, left_one, left_one_t, left_two_t)
    return results[:n], results[n:]


def middle_rest(x, back, hid, back_pre, left_two, n, me):
    units, width, tokens = x.shape

    def body(me_ref, x_ref, c_ref, hid_ref, bp_ref, two_ref, *refs):
        outs, grad_ref, mix_o = refs[:n], refs[n], refs[n + 1]
        for pair in range(STEP // 2):
            values = []
            for h in range(2):
                i = pair * 2 + h
                values.append(dot(two_ref[i], hid_ref[i], 1, 0))
                grads = [dot(bp_ref[i], x_ref[i], 1, 1), dot(c_ref[i], hid_ref[i], 1, 1)]
                grad_ref[i] = jnp.concatenate(grads, axis=1).astype(BF)
            spread_pair(values, outs, pair, me_ref, mix_o)

    piece = pl.BlockSpec((STEP * 8, tokens), lambda g: (g, 0))
    weights = pl.BlockSpec((STEP, width, width), lambda g: (g, 0, 0))
    local = pl.BlockSpec((STEP, width, tokens), lambda g: (g, 0, 0))
    results = pl.pallas_call(
        body,
        grid=(units // STEP,),
        in_specs=[pl.BlockSpec(memory_space=pltpu.SMEM)] + [local] * 4 + [weights],
        out_specs=[piece] * n + [pl.BlockSpec((STEP, width, 2 * width), lambda g: (g, 0, 0))],
        out_shape=[jax.ShapeDtypeStruct((units * 8, tokens), BF)] * n
        + [jax.ShapeDtypeStruct((units, width, 2 * width), BF)],
        scratch_shapes=[pltpu.VMEM((2, width, tokens), F32)],
        compiler_params=params(),
        name="middle_rest",
    )(me, x, back, hid, back_pre, left_two)
    return results[:n], results[n]


def load_wide(pieces, me_ref, wide_ref):
    rows = pieces[0].shape[0]

    @pl.when(pl.program_id(0) == 0)
    def _():
        for d, ref in enumerate(pieces):
            start = pl.multiple_of((me_ref[0] ^ d) * rows, rows)
            for c in range(wide_ref.shape[0]):
                wide_ref[c, pl.ds(start, rows), :] = ref[:, c * 128 : (c + 1) * 128].astype(F32)


def pick_block(wide_ref, hidden, blocks):
    rows = pl.ds(pl.program_id(0), hidden, stride=blocks)
    parts = [wide_ref[c, rows, :].astype(BF) for c in range(wide_ref.shape[0])]
    return jnp.concatenate(parts, axis=1)


def output_side(act, zed, cot, right_two, me):
    n = len(act)
    rows, tokens = act[0].shape
    blocks, feats, hidden = right_two.shape

    def body(me_ref, *refs):
        z_ref, g_ref, w_ref, out_ref, r2_ref, wide_ref = refs[n:]
        load_wide(refs[:n], me_ref, wide_ref)
        mine = pick_block(wide_ref, hidden, blocks)
        last = dot(w_ref[0], mine, 1, 0)
        out_ref[...] = (z_ref[...].astype(F32) + last.T).astype(BF)
        r2_ref[0] = dot(g_ref[...], mine, 0, 1).astype(BF)

    column = pl.BlockSpec((tokens, feats), lambda b: (0, b))
    return pl.pallas_call(
        body,
        grid=(blocks,),
        in_specs=[pl.BlockSpec(memory_space=pltpu.SMEM)]
        + [pl.BlockSpec((rows, tokens), lambda b: (0, 0))] * n
        + [
            column,
            column,
            pl.BlockSpec((1, feats, hidden), lambda b: (b, 0, 0)),
        ],
        out_specs=[column, pl.BlockSpec((1, feats, hidden), lambda b: (b, 0, 0))],
        out_shape=[
            jax.ShapeDtypeStruct(zed.shape, BF),
            jax.ShapeDtypeStruct(right_two.shape, BF),
        ],
        scratch_shapes=[pltpu.VMEM((tokens // 128, n * rows, 128), F32)],
        compiler_params=params(),
        name="output_side",
    )(me, *act, zed, cot, right_two)


def input_side(act, zed, cot, mixed, gain, right_one_t, me):
    n = len(act)
    rows, tokens = act[0].shape
    blocks, feats, hidden = right_one_t.shape

    def body(me_ref, *refs):
        z_ref, g_ref, m_ref, s_ref, w_ref, bz_ref, bm_ref, r1_ref, wide_ref = refs[n:]
        load_wide(refs[:n], me_ref, wide_ref)
        mine = pick_block(wide_ref, hidden, blocks)
        back_z = g_ref[...].astype(F32) + dot(w_ref[0], mine, 1, 0).T
        bz_ref[...] = back_z
        bm_ref[...] = (back_z * s_ref[...]).astype(BF)
        gain_part = jnp.sum(back_z * m_ref[...].astype(F32), axis=0, keepdims=True)
        high = gain_part.astype(BF).astype(F32)
        row = lax.broadcasted_iota(jnp.int32, (8, feats), 0)
        tail = jnp.where(row == 0, high, jnp.where(row == 1, gain_part - high, 0.0)).astype(BF)
        grad = dot(mine, z_ref[...], 1, 0).astype(BF)
        for h in range(2):
            r1_ref[h, : hidden // 2, :] = grad[h * hidden // 2 : (h + 1) * hidden // 2]
            r1_ref[h, hidden // 2 :, :] = tail

    column = pl.BlockSpec((tokens, feats), lambda b: (0, b))
    row = pl.BlockSpec((1, feats), lambda b: (0, b))
    return pl.pallas_call(
        body,
        grid=(blocks,),
        in_specs=[pl.BlockSpec(memory_space=pltpu.SMEM)]
        + [pl.BlockSpec((rows, tokens), lambda b: (0, 0))] * n
        + [
            column,
            column,
            column,
            row,
            pl.BlockSpec((1, feats, hidden), lambda b: (b, 0, 0)),
        ],
        out_specs=[
            column,
            column,
            pl.BlockSpec((2, hidden // 2 + 8, feats), lambda b: (b, 0, 0)),
        ],
        out_shape=[
            jax.ShapeDtypeStruct(zed.shape, F32),
            jax.ShapeDtypeStruct(zed.shape, BF),
            jax.ShapeDtypeStruct((blocks * 2, hidden // 2 + 8, feats), BF),
        ],
        scratch_shapes=[pltpu.VMEM((tokens // 128, n * rows, 128), F32)],
        compiler_params=params(),
        name="input_side",
    )(me, *act, zed, cot, mixed, gain, right_one_t)


def per_device(
    tokens, cotangent, seq_right, seq_left, seq_gain, right_one, left_one, left_two, right_two
):
    rows_here, cols_here = tokens.shape
    block_len = seq_right.shape[1]
    blocks_here = rows_here // block_len
    n_mp = lax.axis_size("mp")
    me = lax.axis_index("mp").astype(jnp.int32)
    me1 = me.reshape(1)
    scale_rows = float(rows_here * lax.axis_size("dp")) ** (-0.5)
    scale_cols = float(cols_here * n_mp) ** (-0.5)

    pieces = expand(cotangent, jnp.swapaxes(right_two, 1, 2), n_mp, me1)
    seq_view = tokens.reshape(blocks_here, block_len, cols_here)
    first = product("sij,sjc->sic", seq_right, seq_view).astype(BF)
    first, pieces = together(first, pieces)
    back_c1 = send(pieces, 2, 6, 1, 3, 7)
    first_moved = lax.all_to_all(first, "dp", split_axis=1, concat_axis=0, tiled=True)
    first_moved, back_c1 = together(first_moved, back_c1)
    mixed_moved = product("isk,kic->sic", seq_left, first_moved).astype(BF)
    back_c2 = send(pieces, 4, 5)
    mixed = lax.all_to_all(mixed_moved, "dp", split_axis=0, concat_axis=1, tiled=True)
    mixed = mixed.reshape(rows_here, cols_here)
    mixed, back_c2 = together(mixed, back_c2)
    back_c = in_order(pieces, back_c1, back_c2)
    zed = (tokens.astype(F32) + seq_gain * mixed.astype(F32)).astype(BF)

    pieces = expand(zed, right_one, n_mp, me1)
    act_a = in_order(pieces, send(pieces, 2, 6, 4, 3, 7, 5, 1))
    pieces, (x, back, hid, back_pre) = middle_main(
        act_a, back_c, left_one, jnp.swapaxes(left_one, 1, 2), jnp.swapaxes(left_two, 1, 2), me1
    )
    back_a1 = send(pieces, 2, 6, 1)
    pieces_c, part_left = middle_rest(x, back, hid, back_pre, left_two, n_mp, me1)
    part_left, back_a1 = together(part_left, back_a1)
    back_a2 = send(pieces, 3, 7, 4)
    slice_left = (sum_slice(part_left) * scale_rows).astype(BF)
    slice_left, back_a2 = together(slice_left, back_a2)
    back_a3 = send(pieces, 5)
    sum_left = all_slices(slice_left)
    sum_left, back_a3 = together(sum_left, back_a3)
    sum_left = sum_left.astype(F32).reshape(part_left.shape)
    back_a = in_order(pieces, back_a1, back_a2, back_a3)

    pieces_c, back_a = together(pieces_c, back_a)
    act_c1 = send(pieces_c, 2, 6)
    back_z, back_mixed, part_r1 = input_side(
        back_a,
        zed,
        cotangent,
        mixed,
        seq_gain.reshape(1, cols_here),
        jnp.swapaxes(right_one, 1, 2),
        me1,
    )
    back_mixed, act_c1 = together(back_mixed, act_c1)
    back_z = back_z.reshape(blocks_here, block_len, cols_here)
    back_mixed = back_mixed.reshape(blocks_here, block_len, cols_here)
    act_c2 = send(pieces_c, 3, 7, 4)
    back_mixed_moved = lax.all_to_all(back_mixed, "dp", split_axis=1, concat_axis=0, tiled=True)
    back_mixed_moved, act_c2 = together(back_mixed_moved, act_c2)
    back_first_moved = product("isk,sic->kic", seq_left, back_mixed_moved).astype(BF)
    part_seq_left = product("sic,kic->isk", back_mixed_moved, first_moved)
    act_c3 = send(pieces_c, 5, 1)
    back_first = lax.all_to_all(back_first_moved, "dp", split_axis=0, concat_axis=1, tiled=True)
    back_first, act_c3 = together(back_first, act_c3)
    act_c = in_order(pieces_c, act_c1, act_c2, act_c3)

    part_r1, back_first = together(part_r1, back_first)
    slice_r1 = sum_slice(part_r1)
    output, part_r2 = output_side(act_c, zed, cotangent, right_two, me1)
    slice_r1, part_r2 = together(slice_r1, part_r2)
    half = right_one.shape[1] // 2
    slice_gain = slice_r1[half : half + 1] + slice_r1[half + 1 : half + 2]
    slice_r1 = jnp.concatenate([slice_r1[:half], jnp.broadcast_to(slice_gain, (8, block_len))])
    slice_r2 = sum_slice(part_r2)
    slice_r1, slice_r2 = together((slice_r1 * scale_rows).astype(BF), (slice_r2 * scale_rows).astype(BF))
    sum_r1 = all_slices(slice_r1).astype(F32)
    sum_r2 = all_slices(slice_r2).astype(F32)

    grad_tokens = (back_z + product("sij,sic->sjc", seq_right, back_first)).astype(BF)
    part_seq_right = product("sic,sjc->sij", back_first, seq_view)
    seq_sum = sum_over_mp(
        jnp.concatenate([part_seq_right.reshape(-1, 128), part_seq_left.reshape(-1, 128)])
    )
    seq_rows = part_seq_right.size // 128
    return (
        output,
        grad_tokens.reshape(rows_here, cols_here),
        seq_sum[:seq_rows].reshape(part_seq_right.shape) * scale_cols,
        seq_sum[seq_rows:].reshape(part_seq_left.shape) * scale_cols,
        sum_r1[::2, half].reshape(cols_here),
        sum_r1[:, :half].reshape(right_one.shape),
        sum_left[:, :, : left_one.shape[2]],
        sum_left[:, :, left_one.shape[2] :],
        sum_r2.reshape(right_two.shape),
    )


def solution(mesh):
    specs = (
        P("dp", "mp"),
        P("dp", "mp"),
        P("dp", None, None),
        P("dp", None, None),
        P("mp"),
        P("mp", None, None),
        P("mp", None, None),
        P("mp", None, None),
        P("mp", None, None),
    )
    return jax.shard_map(per_device, mesh=mesh, in_specs=specs, out_specs=specs, check_vma=False)
```

```python
import math

import jax
import jax.numpy as jnp
from jax import lax
from jax.experimental import pallas as pl
from jax.experimental.pallas import tpu as pltpu
from jax.sharding import PartitionSpec as P

BF = jnp.bfloat16
F32 = jnp.float32
VMEM_BYTES = 56 * 1024 * 1024


def dot(left_arg, right_arg, left_dim, right_dim):
    return lax.dot_general(
        left_arg,
        right_arg,
        (((left_dim,), (right_dim,)), ((), ())),
        preferred_element_type=F32,
    )


def product(form, left_arg, right_arg):
    return jnp.einsum(form, left_arg, right_arg, preferred_element_type=F32)


def slice_parts(parts):
    n = lax.axis_size("dp")
    parts = parts.reshape(n, -1, parts.shape[-1])
    return lax.all_to_all(parts, "dp", split_axis=0, concat_axis=0, tiled=True)


def add_parts(parts, scale):
    return jnp.sum(parts.astype(F32), axis=0) * scale


def all_slices(piece):
    n = lax.axis_size("dp")
    copies = jnp.broadcast_to(piece[None], (n,) + piece.shape)
    return lax.all_to_all(copies, "dp", split_axis=0, concat_axis=0, tiled=True)


def sum_over_mp(value):
    n = lax.axis_size("mp")
    core = lax.axis_index("mp") % 2
    half = value.shape[0] // 2
    halves = value.reshape(2, half, value.shape[1])
    mine = lax.dynamic_index_in_dim(halves, core, 0, keepdims=False)
    other = lax.dynamic_index_in_dim(halves, 1 - core, 0, keepdims=False)
    swap = [(i, i ^ 1) for i in range(n)]
    mine = mine + lax.ppermute(other, "mp", swap)
    total = mine
    for d in range(2, n, 2):
        total = total + lax.ppermute(mine, "mp", [(i, i ^ d) for i in range(n)])
    other = lax.ppermute(total, "mp", swap)
    return jnp.where(core == 0, jnp.concatenate([total, other]), jnp.concatenate([other, total]))


def params():
    return pltpu.CompilerParams(vmem_limit_bytes=VMEM_BYTES)


def expand(x, weight, parts, me):
    blocks, hidden, feats = weight.shape
    tokens = x.shape[0]
    lanes = tokens // 128
    rows = hidden // parts * blocks

    def body(me_ref, x_ref, w_ref, *refs):
        outs, wide_ref = refs[:parts], refs[parts]
        for b in range(blocks):
            part = dot(w_ref[b], x_ref[:, b * feats : (b + 1) * feats], 1, 1)
            for c in range(lanes):
                wide_ref[c, pl.ds(b, hidden, stride=blocks), :] = part[:, c * 128 : (c + 1) * 128]
        for d in range(parts):
            start = pl.multiple_of((me_ref[0] ^ d) * rows, rows)
            for c in range(lanes):
                outs[d][:, c * 128 : (c + 1) * 128] = wide_ref[c, pl.ds(start, rows), :].astype(BF)

    return pl.pallas_call(
        body,
        in_specs=[pl.BlockSpec(memory_space=pltpu.SMEM)] + [pl.BlockSpec(memory_space=pltpu.VMEM)] * 2,
        out_specs=[pl.BlockSpec(memory_space=pltpu.VMEM)] * parts,
        out_shape=[jax.ShapeDtypeStruct((rows, tokens), BF)] * parts,
        scratch_shapes=[pltpu.VMEM((lanes, hidden * blocks, 128), F32)],
        compiler_params=params(),
        name="expand",
    )(me, x, weight)


def send(pieces, *which):
    n = len(pieces)
    return {d: lax.ppermute(pieces[d], "mp", [(i, i ^ d) for i in range(n)]) for d in which}


def together(*values):
    return lax.optimization_barrier(values)


def in_order(pieces, *groups):
    got = {0: pieces[0]}
    for group in groups:
        got.update(group)
    return [got[d] for d in range(len(pieces))]


STEP = 8


def gather_pair(refs, pair, me_ref, mix_ref):
    for d, ref in enumerate(refs):
        wide = ref[pair * 16 : pair * 16 + 16, :].astype(F32)
        at = pl.multiple_of((me_ref[0] ^ d) * 8, 8)
        for h in range(2):
            mix_ref[h, pl.ds(at, 8), :] = wide[h * 8 : h * 8 + 8]
    return [mix_ref[h].astype(BF) for h in range(2)]


def spread_pair(values, refs, pair, me_ref, mix_ref):
    for h in range(2):
        mix_ref[h] = values[h]
    for d, ref in enumerate(refs):
        at = pl.multiple_of((me_ref[0] ^ d) * 8, 8)
        block = jnp.concatenate([mix_ref[h, pl.ds(at, 8), :] for h in range(2)], axis=0)
        ref[pair * 16 : pair * 16 + 16, :] = block.astype(BF)


def middle_main(act, back, left_one, left_one_t, left_two_t, me):
    n = len(act)
    tokens = act[0].shape[1]
    units, width, _ = left_one.shape

    def body(me_ref, *refs):
        acts, backs, (one_ref, one_t_ref, two_t_ref) = refs[:n], refs[n : 2 * n], refs[2 * n : 2 * n + 3]
        outs = refs[2 * n + 3 : 3 * n + 3]
        x_ref, c_ref, hid_ref, bp_ref, mix_a, mix_c, mix_o = refs[3 * n + 3 :]
        for pair in range(STEP // 2):
            xs = gather_pair(acts, pair, me_ref, mix_a)
            cs = gather_pair(backs, pair, me_ref, mix_c)
            values = []
            for h in range(2):
                i = pair * 2 + h
                pre = dot(one_ref[i], xs[h], 1, 0)
                back_h = dot(two_t_ref[i], cs[h], 1, 0)
                cdf = 0.5 * (1.0 + lax.erf(pre * (1.0 / math.sqrt(2.0))))
                slope = cdf + pre * jnp.exp(-0.5 * pre * pre) * (1.0 / math.sqrt(2.0 * math.pi))
                back_pre = (back_h * slope).astype(BF)
                x_ref[i] = xs[h]
                c_ref[i] = cs[h]
                hid_ref[i] = (pre * cdf).astype(BF)
                bp_ref[i] = back_pre
                values.append(dot(one_t_ref[i], back_pre, 1, 0))
            spread_pair(values, outs, pair, me_ref, mix_o)

    piece = pl.BlockSpec((STEP * 8, tokens), lambda g: (g, 0))
    weights = pl.BlockSpec((STEP, width, width), lambda g: (g, 0, 0))
    local = pl.BlockSpec((STEP, width, tokens), lambda g: (g, 0, 0))
    results = pl.pallas_call(
        body,
        grid=(units // STEP,),
        in_specs=[pl.BlockSpec(memory_space=pltpu.SMEM)] + [piece] * (2 * n) + [weights] * 3,
        out_specs=[piece] * n + [local] * 4,
        out_shape=[jax.ShapeDtypeStruct(act[0].shape, BF)] * n
        + [jax.ShapeDtypeStruct((units, width, tokens), BF)] * 4,
        scratch_shapes=[pltpu.VMEM((2, width, tokens), F32)] * 3,
        compiler_params=params(),
        name="middle_main",
    )(me, *act, *back, left_one, left_one_t, left_two_t)
    return results[:n], results[n:]


def middle_rest(x, back, hid, back_pre, left_two, n, me):
    units, width, tokens = x.shape

    def body(me_ref, x_ref, c_ref, hid_ref, bp_ref, two_ref, *refs):
        outs, grad_ref, mix_o = refs[:n], refs[n], refs[n + 1]
        for pair in range(STEP // 2):
            values = []
            for h in range(2):
                i = pair * 2 + h
                values.append(dot(two_ref[i], hid_ref[i], 1, 0))
                grads = [dot(bp_ref[i], x_ref[i], 1, 1), dot(c_ref[i], hid_ref[i], 1, 1)]
                grad_ref[i] = jnp.concatenate(grads, axis=1).astype(BF)
            spread_pair(values, outs, pair, me_ref, mix_o)

    piece = pl.BlockSpec((STEP * 8, tokens), lambda g: (g, 0))
    weights = pl.BlockSpec((STEP, width, width), lambda g: (g, 0, 0))
    local = pl.BlockSpec((STEP, width, tokens), lambda g: (g, 0, 0))
    results = pl.pallas_call(
        body,
        grid=(units // STEP,),
        in_specs=[pl.BlockSpec(memory_space=pltpu.SMEM)] + [local] * 4 + [weights],
        out_specs=[piece] * n + [pl.BlockSpec((STEP, width, 2 * width), lambda g: (g, 0, 0))],
        out_shape=[jax.ShapeDtypeStruct((units * 8, tokens), BF)] * n
        + [jax.ShapeDtypeStruct((units, width, 2 * width), BF)],
        scratch_shapes=[pltpu.VMEM((2, width, tokens), F32)],
        compiler_params=params(),
        name="middle_rest",
    )(me, x, back, hid, back_pre, left_two)
    return results[:n], results[n]


def load_wide(pieces, me_ref, wide_ref):
    rows = pieces[0].shape[0]

    @pl.when(pl.program_id(0) == 0)
    def _():
        for d, ref in enumerate(pieces):
            start = pl.multiple_of((me_ref[0] ^ d) * rows, rows)
            for c in range(wide_ref.shape[0]):
                wide_ref[c, pl.ds(start, rows), :] = ref[:, c * 128 : (c + 1) * 128].astype(F32)


def pick_block(wide_ref, hidden, blocks):
    rows = pl.ds(pl.program_id(0), hidden, stride=blocks)
    parts = [wide_ref[c, rows, :].astype(BF) for c in range(wide_ref.shape[0])]
    return jnp.concatenate(parts, axis=1)


def output_side(act, zed, cot, right_two, me):
    n = len(act)
    rows, tokens = act[0].shape
    blocks, feats, hidden = right_two.shape

    def body(me_ref, *refs):
        z_ref, g_ref, w_ref, out_ref, r2_ref, wide_ref = refs[n:]
        load_wide(refs[:n], me_ref, wide_ref)
        mine = pick_block(wide_ref, hidden, blocks)
        last = dot(w_ref[0], mine, 1, 0)
        out_ref[...] = (z_ref[...].astype(F32) + last.T).astype(BF)
        r2_ref[0] = dot(g_ref[...], mine, 0, 1).astype(BF)

    column = pl.BlockSpec((tokens, feats), lambda b: (0, b))
    return pl.pallas_call(
        body,
        grid=(blocks,),
        in_specs=[pl.BlockSpec(memory_space=pltpu.SMEM)]
        + [pl.BlockSpec((rows, tokens), lambda b: (0, 0))] * n
        + [
            column,
            column,
            pl.BlockSpec((1, feats, hidden), lambda b: (b, 0, 0)),
        ],
        out_specs=[column, pl.BlockSpec((1, feats, hidden), lambda b: (b, 0, 0))],
        out_shape=[
            jax.ShapeDtypeStruct(zed.shape, BF),
            jax.ShapeDtypeStruct(right_two.shape, BF),
        ],
        scratch_shapes=[pltpu.VMEM((tokens // 128, n * rows, 128), F32)],
        compiler_params=params(),
        name="output_side",
    )(me, *act, zed, cot, right_two)


def input_side(act, zed, cot, mixed, gain, right_one_t, me):
    n = len(act)
    rows, tokens = act[0].shape
    blocks, feats, hidden = right_one_t.shape

    def body(me_ref, *refs):
        z_ref, g_ref, m_ref, s_ref, w_ref, bz_ref, bm_ref, r1_ref, wide_ref = refs[n:]
        load_wide(refs[:n], me_ref, wide_ref)
        mine = pick_block(wide_ref, hidden, blocks)
        back_z = g_ref[...].astype(F32) + dot(w_ref[0], mine, 1, 0).T
        bz_ref[...] = back_z
        bm_ref[...] = (back_z * s_ref[...]).astype(BF)
        gain_part = jnp.sum(back_z * m_ref[...].astype(F32), axis=0, keepdims=True)
        high = gain_part.astype(BF).astype(F32)
        row = lax.broadcasted_iota(jnp.int32, (8, feats), 0)
        tail = jnp.where(row == 0, high, jnp.where(row == 1, gain_part - high, 0.0)).astype(BF)
        grad = dot(mine, z_ref[...], 1, 0).astype(BF)
        for h in range(2):
            r1_ref[h, : hidden // 2, :] = grad[h * hidden // 2 : (h + 1) * hidden // 2]
            r1_ref[h, hidden // 2 :, :] = tail

    column = pl.BlockSpec((tokens, feats), lambda b: (0, b))
    row = pl.BlockSpec((1, feats), lambda b: (0, b))
    return pl.pallas_call(
        body,
        grid=(blocks,),
        in_specs=[pl.BlockSpec(memory_space=pltpu.SMEM)]
        + [pl.BlockSpec((rows, tokens), lambda b: (0, 0))] * n
        + [
            column,
            column,
            column,
            row,
            pl.BlockSpec((1, feats, hidden), lambda b: (b, 0, 0)),
        ],
        out_specs=[
            column,
            column,
            pl.BlockSpec((2, hidden // 2 + 8, feats), lambda b: (b, 0, 0)),
        ],
        out_shape=[
            jax.ShapeDtypeStruct(zed.shape, F32),
            jax.ShapeDtypeStruct(zed.shape, BF),
            jax.ShapeDtypeStruct((blocks * 2, hidden // 2 + 8, feats), BF),
        ],
        scratch_shapes=[pltpu.VMEM((tokens // 128, n * rows, 128), F32)],
        compiler_params=params(),
        name="input_side",
    )(me, *act, zed, cot, mixed, gain, right_one_t)


def per_device(
    tokens, cotangent, seq_right, seq_left, seq_gain, right_one, left_one, left_two, right_two
):
    rows_here, cols_here = tokens.shape
    block_len = seq_right.shape[1]
    blocks_here = rows_here // block_len
    n_mp = lax.axis_size("mp")
    me = lax.axis_index("mp").astype(jnp.int32)
    me1 = me.reshape(1)
    scale_rows = float(rows_here * lax.axis_size("dp")) ** (-0.5)
    scale_cols = float(cols_here * n_mp) ** (-0.5)

    pieces = expand(cotangent, jnp.swapaxes(right_two, 1, 2), n_mp, me1)
    seq_view = tokens.reshape(blocks_here, block_len, cols_here)
    first = product("sij,sjc->sic", seq_right, seq_view).astype(BF)
    first, pieces = together(first, pieces)
    back_c1 = send(pieces, 2, 6, 1, 3, 7)
    first_moved = lax.all_to_all(first, "dp", split_axis=1, concat_axis=0, tiled=True)
    first_moved, back_c1 = together(first_moved, back_c1)
    mixed_moved = product("isk,kic->sic", seq_left, first_moved).astype(BF)
    back_c2 = send(pieces, 4, 5)
    mixed = lax.all_to_all(mixed_moved, "dp", split_axis=0, concat_axis=1, tiled=True)
    mixed = mixed.reshape(rows_here, cols_here)
    mixed, back_c2 = together(mixed, back_c2)
    back_c = in_order(pieces, back_c1, back_c2)
    zed = (tokens.astype(F32) + seq_gain * mixed.astype(F32)).astype(BF)

    pieces = expand(zed, right_one, n_mp, me1)
    act_a = in_order(pieces, send(pieces, 2, 6, 4, 3, 7, 5, 1))
    pieces, (x, back, hid, back_pre) = middle_main(
        act_a, back_c, left_one, jnp.swapaxes(left_one, 1, 2), jnp.swapaxes(left_two, 1, 2), me1
    )
    back_a1 = send(pieces, 2, 6, 1)
    pieces_c, part_left = middle_rest(x, back, hid, back_pre, left_two, n_mp, me1)
    part_left, back_a1 = together(part_left, back_a1)
    back_a2 = send(pieces, 3, 7, 4, 5)
    back_a = in_order(pieces, back_a1, back_a2)
    left_parts = slice_parts(part_left)

    pieces_c, back_a = together(pieces_c, back_a)
    act_c1 = send(pieces_c, 2, 6)
    back_z, back_mixed, part_r1 = input_side(
        back_a,
        zed,
        cotangent,
        mixed,
        seq_gain.reshape(1, cols_here),
        jnp.swapaxes(right_one, 1, 2),
        me1,
    )
    back_mixed, act_c1, left_parts = together(back_mixed, act_c1, left_parts)
    back_z = back_z.reshape(blocks_here, block_len, cols_here)
    back_mixed = back_mixed.reshape(blocks_here, block_len, cols_here)
    act_c2 = send(pieces_c, 3, 7)
    back_mixed_moved = lax.all_to_all(back_mixed, "dp", split_axis=1, concat_axis=0, tiled=True)
    back_mixed_moved, act_c2, part_r1 = together(back_mixed_moved, act_c2, part_r1)
    back_first_moved = product("isk,sic->kic", seq_left, back_mixed_moved).astype(BF)
    part_seq_left = product("sic,kic->isk", back_mixed_moved, first_moved)
    act_c3 = send(pieces_c, 4, 1)
    r1_parts = slice_parts(part_r1)
    back_first_moved, r1_parts, act_c3 = together(back_first_moved, r1_parts, act_c3)
    act_c4 = send(pieces_c, 5)
    back_first = lax.all_to_all(back_first_moved, "dp", split_axis=0, concat_axis=1, tiled=True)
    act_c = in_order(pieces_c, act_c1, act_c2, act_c3, act_c4)
    slice_left = add_parts(left_parts, scale_rows)
    slice_r1 = add_parts(r1_parts, scale_rows)
    half = right_one.shape[1] // 2
    slice_gain = slice_r1[half : half + 1] + slice_r1[half + 1 : half + 2]
    slice_gain = jnp.broadcast_to(slice_gain, (8, block_len))
    slices = jnp.concatenate([slice_left, slice_r1[:half], slice_gain]).astype(BF)
    rows_left = slice_left.shape[0]
    gathered = lax.all_gather(slices, "dp")

    output, part_r2 = output_side(act_c, zed, cotangent, right_two, me1)
    back_first, part_r2 = together(back_first, part_r2)
    slice_r2 = add_parts(slice_parts(part_r2), scale_rows).astype(BF)
    slice_r2, gathered = together(slice_r2, gathered)
    gathered = gathered.astype(F32)
    sum_left = gathered[:, :rows_left].reshape(part_left.shape)
    sum_r1 = gathered[:, rows_left : rows_left + half].reshape(right_one.shape)
    sum_gain = gathered[::2, rows_left + half].reshape(cols_here)
    sum_r2 = all_slices(slice_r2).astype(F32)

    grad_tokens = (back_z + product("sij,sic->sjc", seq_right, back_first)).astype(BF)
    part_seq_right = product("sic,sjc->sij", back_first, seq_view)
    seq_sum = sum_over_mp(
        jnp.concatenate([part_seq_right.reshape(-1, 128), part_seq_left.reshape(-1, 128)])
    )
    seq_rows = part_seq_right.size // 128
    return (
        output,
        grad_tokens.reshape(rows_here, cols_here),
        seq_sum[:seq_rows].reshape(part_seq_right.shape) * scale_cols,
        seq_sum[seq_rows:].reshape(part_seq_left.shape) * scale_cols,
        sum_gain,
        sum_r1,
        sum_left[:, :, : left_one.shape[2]],
        sum_left[:, :, left_one.shape[2] :],
        sum_r2.reshape(right_two.shape),
    )


def solution(mesh):
    specs = (
        P("dp", "mp"),
        P("dp", "mp"),
        P("dp", None, None),
        P("dp", None, None),
        P("mp"),
        P("mp", None, None),
        P("mp", None, None),
        P("mp", None, None),
        P("mp", None, None),
    )
    return jax.shard_map(per_device, mesh=mesh, in_specs=specs, out_specs=specs, check_vma=False)
```

```python
import math

import jax
import jax.numpy as jnp
from jax import lax
from jax.experimental import pallas as pl
from jax.experimental.pallas import tpu as pltpu
from jax.sharding import PartitionSpec as P

BF = jnp.bfloat16
F32 = jnp.float32
VMEM_BYTES = 56 * 1024 * 1024


def dot(left_arg, right_arg, left_dim, right_dim):
    return lax.dot_general(
        left_arg,
        right_arg,
        (((left_dim,), (right_dim,)), ((), ())),
        preferred_element_type=F32,
    )


def product(form, left_arg, right_arg):
    return jnp.einsum(form, left_arg, right_arg, preferred_element_type=F32)


def slice_parts(parts):
    n = lax.axis_size("dp")
    parts = parts.reshape(n, -1, parts.shape[-1])
    return lax.all_to_all(parts, "dp", split_axis=0, concat_axis=0, tiled=True)


def add_parts(parts, scale):
    return jnp.sum(parts.astype(F32), axis=0) * scale


def all_slices(piece):
    n = lax.axis_size("dp")
    copies = jnp.broadcast_to(piece[None], (n,) + piece.shape)
    return lax.all_to_all(copies, "dp", split_axis=0, concat_axis=0, tiled=True)


def sum_over_mp(value):
    n = lax.axis_size("mp")
    core = lax.axis_index("mp") % 2
    half = value.shape[0] // 2
    halves = value.reshape(2, half, value.shape[1])
    mine = lax.dynamic_index_in_dim(halves, core, 0, keepdims=False)
    other = lax.dynamic_index_in_dim(halves, 1 - core, 0, keepdims=False)
    swap = [(i, i ^ 1) for i in range(n)]
    mine = mine + lax.ppermute(other, "mp", swap)
    total = mine
    for d in range(2, n, 2):
        total = total + lax.ppermute(mine, "mp", [(i, i ^ d) for i in range(n)])
    other = lax.ppermute(total, "mp", swap)
    return jnp.where(core == 0, jnp.concatenate([total, other]), jnp.concatenate([other, total]))


def params():
    return pltpu.CompilerParams(vmem_limit_bytes=VMEM_BYTES)


def expand(x, weight, parts, me):
    blocks, hidden, feats = weight.shape
    tokens = x.shape[0]
    lanes = tokens // 128
    rows = hidden // parts * blocks

    def body(me_ref, x_ref, w_ref, *refs):
        outs, wide_ref = refs[:parts], refs[parts]
        for b in range(blocks):
            part = dot(w_ref[b], x_ref[:, b * feats : (b + 1) * feats], 1, 1)
            for c in range(lanes):
                wide_ref[c, pl.ds(b, hidden, stride=blocks), :] = part[:, c * 128 : (c + 1) * 128]
        for d in range(parts):
            start = pl.multiple_of((me_ref[0] ^ d) * rows, rows)
            for c in range(lanes):
                outs[d][:, c * 128 : (c + 1) * 128] = wide_ref[c, pl.ds(start, rows), :].astype(BF)

    return pl.pallas_call(
        body,
        in_specs=[pl.BlockSpec(memory_space=pltpu.SMEM)] + [pl.BlockSpec(memory_space=pltpu.VMEM)] * 2,
        out_specs=[pl.BlockSpec(memory_space=pltpu.VMEM)] * parts,
        out_shape=[jax.ShapeDtypeStruct((rows, tokens), BF)] * parts,
        scratch_shapes=[pltpu.VMEM((lanes, hidden * blocks, 128), F32)],
        compiler_params=params(),
        name="expand",
    )(me, x, weight)


def send(pieces, *which):
    n = len(pieces)
    return {d: lax.ppermute(pieces[d], "mp", [(i, i ^ d) for i in range(n)]) for d in which}


def together(*values):
    return lax.optimization_barrier(values)


def in_order(pieces, *groups):
    got = {0: pieces[0]}
    for group in groups:
        got.update(group)
    return [got[d] for d in range(len(pieces))]


STEP = 8


def gather_pair(refs, pair, me_ref, mix_ref):
    for d, ref in enumerate(refs):
        wide = ref[pair * 16 : pair * 16 + 16, :].astype(F32)
        at = pl.multiple_of((me_ref[0] ^ d) * 8, 8)
        for h in range(2):
            mix_ref[h, pl.ds(at, 8), :] = wide[h * 8 : h * 8 + 8]
    return [mix_ref[h].astype(BF) for h in range(2)]


def spread_pair(values, refs, pair, me_ref, mix_ref):
    for h in range(2):
        mix_ref[h] = values[h]
    for d, ref in enumerate(refs):
        at = pl.multiple_of((me_ref[0] ^ d) * 8, 8)
        block = jnp.concatenate([mix_ref[h, pl.ds(at, 8), :] for h in range(2)], axis=0)
        ref[pair * 16 : pair * 16 + 16, :] = block.astype(BF)


def middle_main(act, back, left_one, left_one_t, left_two_t, me):
    n = len(act)
    tokens = act[0].shape[1]
    units, width, _ = left_one.shape

    def body(me_ref, *refs):
        acts, backs, (one_ref, one_t_ref, two_t_ref) = refs[:n], refs[n : 2 * n], refs[2 * n : 2 * n + 3]
        outs = refs[2 * n + 3 : 3 * n + 3]
        x_ref, c_ref, hid_ref, bp_ref, mix_a, mix_c, mix_o = refs[3 * n + 3 :]
        for pair in range(STEP // 2):
            xs = gather_pair(acts, pair, me_ref, mix_a)
            cs = gather_pair(backs, pair, me_ref, mix_c)
            values = []
            for h in range(2):
                i = pair * 2 + h
                pre = dot(one_ref[i], xs[h], 1, 0)
                back_h = dot(two_t_ref[i], cs[h], 1, 0)
                cdf = 0.5 * (1.0 + lax.erf(pre * (1.0 / math.sqrt(2.0))))
                slope = cdf + pre * jnp.exp(-0.5 * pre * pre) * (1.0 / math.sqrt(2.0 * math.pi))
                back_pre = (back_h * slope).astype(BF)
                x_ref[i] = xs[h]
                c_ref[i] = cs[h]
                hid_ref[i] = (pre * cdf).astype(BF)
                bp_ref[i] = back_pre
                values.append(dot(one_t_ref[i], back_pre, 1, 0))
            spread_pair(values, outs, pair, me_ref, mix_o)

    piece = pl.BlockSpec((STEP * 8, tokens), lambda g: (g, 0))
    weights = pl.BlockSpec((STEP, width, width), lambda g: (g, 0, 0))
    local = pl.BlockSpec((STEP, width, tokens), lambda g: (g, 0, 0))
    results = pl.pallas_call(
        body,
        grid=(units // STEP,),
        in_specs=[pl.BlockSpec(memory_space=pltpu.SMEM)] + [piece] * (2 * n) + [weights] * 3,
        out_specs=[piece] * n + [local] * 4,
        out_shape=[jax.ShapeDtypeStruct(act[0].shape, BF)] * n
        + [jax.ShapeDtypeStruct((units, width, tokens), BF)] * 4,
        scratch_shapes=[pltpu.VMEM((2, width, tokens), F32)] * 3,
        compiler_params=params(),
        name="middle_main",
    )(me, *act, *back, left_one, left_one_t, left_two_t)
    return results[:n], results[n:]


def middle_rest(x, back, hid, back_pre, left_two, n, me):
    units, width, tokens = x.shape

    def body(me_ref, x_ref, c_ref, hid_ref, bp_ref, two_ref, *refs):
        outs, grad_ref, mix_o = refs[:n], refs[n], refs[n + 1]
        for pair in range(STEP // 2):
            values = []
            for h in range(2):
                i = pair * 2 + h
                values.append(dot(two_ref[i], hid_ref[i], 1, 0))
                grads = [dot(bp_ref[i], x_ref[i], 1, 1), dot(c_ref[i], hid_ref[i], 1, 1)]
                grad_ref[i] = jnp.concatenate(grads, axis=1).astype(BF)
            spread_pair(values, outs, pair, me_ref, mix_o)

    piece = pl.BlockSpec((STEP * 8, tokens), lambda g: (g, 0))
    weights = pl.BlockSpec((STEP, width, width), lambda g: (g, 0, 0))
    local = pl.BlockSpec((STEP, width, tokens), lambda g: (g, 0, 0))
    results = pl.pallas_call(
        body,
        grid=(units // STEP,),
        in_specs=[pl.BlockSpec(memory_space=pltpu.SMEM)] + [local] * 4 + [weights],
        out_specs=[piece] * n + [pl.BlockSpec((STEP, width, 2 * width), lambda g: (g, 0, 0))],
        out_shape=[jax.ShapeDtypeStruct((units * 8, tokens), BF)] * n
        + [jax.ShapeDtypeStruct((units, width, 2 * width), BF)],
        scratch_shapes=[pltpu.VMEM((2, width, tokens), F32)],
        compiler_params=params(),
        name="middle_rest",
    )(me, x, back, hid, back_pre, left_two)
    return results[:n], results[n]


def load_wide(pieces, me_ref, wide_ref):
    rows = pieces[0].shape[0]

    @pl.when(pl.program_id(0) == 0)
    def _():
        for d, ref in enumerate(pieces):
            start = pl.multiple_of((me_ref[0] ^ d) * rows, rows)
            for c in range(wide_ref.shape[0]):
                wide_ref[c, pl.ds(start, rows), :] = ref[:, c * 128 : (c + 1) * 128].astype(F32)


def pick_block(wide_ref, hidden, blocks):
    rows = pl.ds(pl.program_id(0), hidden, stride=blocks)
    parts = [wide_ref[c, rows, :].astype(BF) for c in range(wide_ref.shape[0])]
    return jnp.concatenate(parts, axis=1)


def output_side(act, zed, cot, right_two, me):
    n = len(act)
    rows, tokens = act[0].shape
    blocks, feats, hidden = right_two.shape

    def body(me_ref, *refs):
        z_ref, g_ref, w_ref, out_ref, r2_ref, wide_ref = refs[n:]
        load_wide(refs[:n], me_ref, wide_ref)
        mine = pick_block(wide_ref, hidden, blocks)
        last = dot(w_ref[0], mine, 1, 0)
        out_ref[...] = (z_ref[...].astype(F32) + last.T).astype(BF)
        r2_ref[0] = dot(g_ref[...], mine, 0, 1).astype(BF)

    column = pl.BlockSpec((tokens, feats), lambda b: (0, b))
    return pl.pallas_call(
        body,
        grid=(blocks,),
        in_specs=[pl.BlockSpec(memory_space=pltpu.SMEM)]
        + [pl.BlockSpec((rows, tokens), lambda b: (0, 0))] * n
        + [
            column,
            column,
            pl.BlockSpec((1, feats, hidden), lambda b: (b, 0, 0)),
        ],
        out_specs=[column, pl.BlockSpec((1, feats, hidden), lambda b: (b, 0, 0))],
        out_shape=[
            jax.ShapeDtypeStruct(zed.shape, BF),
            jax.ShapeDtypeStruct(right_two.shape, BF),
        ],
        scratch_shapes=[pltpu.VMEM((tokens // 128, n * rows, 128), F32)],
        compiler_params=params(),
        name="output_side",
    )(me, *act, zed, cot, right_two)


def by_residue(value, shape):
    parts, rows, cols = shape
    value = value.reshape(rows // 8, parts, 8, cols)
    moved = [value[:, p].reshape(rows, cols)[None] for p in range(parts)]
    return jnp.concatenate(moved, axis=0).astype(BF)


def input_side(act, zed, cot, mixed, gain, right_one_t, n_dp, me):
    n = len(act)
    rows, tokens = act[0].shape
    blocks, feats, hidden = right_one_t.shape

    def body(me_ref, *refs):
        z_ref, g_ref, m_ref, s_ref, w_ref, bz_ref, bm_ref, r1_ref, wide_ref = refs[n:]
        load_wide(refs[:n], me_ref, wide_ref)
        mine = pick_block(wide_ref, hidden, blocks)
        back_z = g_ref[...].astype(F32) + dot(w_ref[0], mine, 1, 0).T
        bz_ref[...] = back_z
        bm_ref[...] = by_residue(back_z * s_ref[...], bm_ref.shape)
        gain_part = jnp.sum(back_z * m_ref[...].astype(F32), axis=0, keepdims=True)
        high = gain_part.astype(BF).astype(F32)
        row = lax.broadcasted_iota(jnp.int32, (8, feats), 0)
        tail = jnp.where(row == 0, high, jnp.where(row == 1, gain_part - high, 0.0)).astype(BF)
        grad = dot(mine, z_ref[...], 1, 0).astype(BF)
        for h in range(2):
            r1_ref[h, : hidden // 2, :] = grad[h * hidden // 2 : (h + 1) * hidden // 2]
            r1_ref[h, hidden // 2 :, :] = tail

    column = pl.BlockSpec((tokens, feats), lambda b: (0, b))
    row = pl.BlockSpec((1, feats), lambda b: (0, b))
    return pl.pallas_call(
        body,
        grid=(blocks,),
        in_specs=[pl.BlockSpec(memory_space=pltpu.SMEM)]
        + [pl.BlockSpec((rows, tokens), lambda b: (0, 0))] * n
        + [
            column,
            column,
            column,
            row,
            pl.BlockSpec((1, feats, hidden), lambda b: (b, 0, 0)),
        ],
        out_specs=[
            column,
            pl.BlockSpec((n_dp, tokens // n_dp, feats), lambda b: (0, 0, b)),
            pl.BlockSpec((2, hidden // 2 + 8, feats), lambda b: (b, 0, 0)),
        ],
        out_shape=[
            jax.ShapeDtypeStruct(zed.shape, F32),
            jax.ShapeDtypeStruct((n_dp, tokens // n_dp, zed.shape[1]), BF),
            jax.ShapeDtypeStruct((blocks * 2, hidden // 2 + 8, feats), BF),
        ],
        scratch_shapes=[pltpu.VMEM((tokens // 128, n * rows, 128), F32)],
        compiler_params=params(),
        name="input_side",
    )(me, *act, zed, cot, mixed, gain, right_one_t)


def per_device(
    tokens, cotangent, seq_right, seq_left, seq_gain, right_one, left_one, left_two, right_two
):
    rows_here, cols_here = tokens.shape
    block_len = seq_right.shape[1]
    blocks_here = rows_here // block_len
    n_mp = lax.axis_size("mp")
    me = lax.axis_index("mp").astype(jnp.int32)
    me1 = me.reshape(1)
    scale_rows = float(rows_here * lax.axis_size("dp")) ** (-0.5)
    scale_cols = float(cols_here * n_mp) ** (-0.5)

    pieces = expand(cotangent, jnp.swapaxes(right_two, 1, 2), n_mp, me1)
    seq_view = tokens.reshape(blocks_here, block_len, cols_here)
    first = product("sij,sjc->sic", seq_right, seq_view).astype(BF)
    first, pieces = together(first, pieces)
    back_c1 = send(pieces, 2, 6, 1, 3, 7)
    first_moved = lax.all_to_all(first, "dp", split_axis=1, concat_axis=0, tiled=True)
    first_moved, back_c1 = together(first_moved, back_c1)
    mixed_moved = product("isk,kic->sic", seq_left, first_moved).astype(BF)
    back_c2 = send(pieces, 4, 5)
    mixed = lax.all_to_all(mixed_moved, "dp", split_axis=0, concat_axis=1, tiled=True)
    mixed = mixed.reshape(rows_here, cols_here)
    mixed, back_c2 = together(mixed, back_c2)
    back_c = in_order(pieces, back_c1, back_c2)
    zed = (tokens.astype(F32) + seq_gain * mixed.astype(F32)).astype(BF)

    pieces = expand(zed, right_one, n_mp, me1)
    act_a = in_order(pieces, send(pieces, 2, 6, 4, 3, 7, 5, 1))
    pieces, (x, back, hid, back_pre) = middle_main(
        act_a, back_c, left_one, jnp.swapaxes(left_one, 1, 2), jnp.swapaxes(left_two, 1, 2), me1
    )
    back_a1 = send(pieces, 2, 6, 3, 7, 1)
    pieces_c, part_left = middle_rest(x, back, hid, back_pre, left_two, n_mp, me1)
    right_one_t = jnp.swapaxes(right_one, 1, 2)
    part_left, back_a1, right_one_t = together(part_left, back_a1, right_one_t)
    back_a2 = send(pieces, 4, 5)
    back_a = in_order(pieces, back_a1, back_a2)
    left_parts = slice_parts(part_left)

    pieces_c, back_a = together(pieces_c, back_a)
    act_c1 = send(pieces_c, 2, 6)
    back_z, back_mixed, part_r1 = input_side(
        back_a,
        zed,
        cotangent,
        mixed,
        seq_gain.reshape(1, cols_here),
        right_one_t,
        lax.axis_size("dp"),
        me1,
    )
    back_mixed, act_c1, left_parts = together(back_mixed, act_c1, left_parts)
    back_z = back_z.reshape(blocks_here, block_len, cols_here)
    act_c2 = send(pieces_c, 3, 7, 1)
    back_mixed_moved = lax.all_to_all(back_mixed, "dp", split_axis=0, concat_axis=0, tiled=True)
    back_mixed_moved = back_mixed_moved.reshape(first_moved.shape)
    back_mixed_moved, act_c2, part_r1 = together(back_mixed_moved, act_c2, part_r1)
    back_first_moved = product("isk,sic->kic", seq_left, back_mixed_moved).astype(BF)
    part_seq_left = product("sic,kic->isk", back_mixed_moved, first_moved)
    act_c3 = send(pieces_c, 4, 5)
    r1_parts = slice_parts(part_r1)
    back_first_moved, r1_parts, act_c3 = together(back_first_moved, r1_parts, act_c3)
    back_first = lax.all_to_all(back_first_moved, "dp", split_axis=0, concat_axis=1, tiled=True)
    act_c = in_order(pieces_c, act_c1, act_c2, act_c3)
    slice_left = add_parts(left_parts, scale_rows)
    slice_r1 = add_parts(r1_parts, scale_rows)
    half = right_one.shape[1] // 2
    slice_gain = slice_r1[half : half + 1] + slice_r1[half + 1 : half + 2]
    slice_gain = jnp.broadcast_to(slice_gain, (8, block_len))
    slices = jnp.concatenate([slice_left, slice_r1[:half], slice_gain]).astype(BF)
    rows_left = slice_left.shape[0]
    gathered = lax.all_gather(slices, "dp")

    output, part_r2 = output_side(act_c, zed, cotangent, right_two, me1)
    back_first, part_r2 = together(back_first, part_r2)
    slice_r2 = add_parts(slice_parts(part_r2), scale_rows).astype(BF)
    sum_r2, gathered = together(all_slices(slice_r2), gathered)
    gathered = gathered.astype(F32)
    sum_left = gathered[:, :rows_left].reshape(part_left.shape)
    sum_r1 = gathered[:, rows_left : rows_left + half].reshape(right_one.shape)
    sum_gain = gathered[::2, rows_left + half].reshape(cols_here)
    sum_r2 = sum_r2.astype(F32)

    grad_tokens = (back_z + product("sij,sic->sjc", seq_right, back_first)).astype(BF)
    part_seq_right = product("sic,sjc->sij", back_first, seq_view)
    seq_sum = sum_over_mp(
        jnp.concatenate([part_seq_right.reshape(-1, 128), part_seq_left.reshape(-1, 128)])
    )
    seq_rows = part_seq_right.size // 128
    return (
        output,
        grad_tokens.reshape(rows_here, cols_here),
        seq_sum[:seq_rows].reshape(part_seq_right.shape) * scale_cols,
        seq_sum[seq_rows:].reshape(part_seq_left.shape) * scale_cols,
        sum_gain,
        sum_r1,
        sum_left[:, :, : left_one.shape[2]],
        sum_left[:, :, left_one.shape[2] :],
        sum_r2.reshape(right_two.shape),
    )


def solution(mesh):
    specs = (
        P("dp", "mp"),
        P("dp", "mp"),
        P("dp", None, None),
        P("dp", None, None),
        P("mp"),
        P("mp", None, None),
        P("mp", None, None),
        P("mp", None, None),
        P("mp", None, None),
    )
    return jax.shard_map(per_device, mesh=mesh, in_specs=specs, out_specs=specs, check_vma=False)
```

```python
import math

import jax
import jax.numpy as jnp
from jax import lax
from jax.experimental import pallas as pl
from jax.experimental.pallas import tpu as pltpu
from jax.sharding import PartitionSpec as P

BF = jnp.bfloat16
F32 = jnp.float32
VMEM_BYTES = 56 * 1024 * 1024


def dot(left_arg, right_arg, left_dim, right_dim):
    return lax.dot_general(
        left_arg,
        right_arg,
        (((left_dim,), (right_dim,)), ((), ())),
        preferred_element_type=F32,
    )


def product(form, left_arg, right_arg):
    return jnp.einsum(form, left_arg, right_arg, preferred_element_type=F32)


def slice_parts(parts):
    n = lax.axis_size("dp")
    parts = parts.reshape(n, -1, parts.shape[-1])
    return lax.all_to_all(parts, "dp", split_axis=0, concat_axis=0, tiled=True)


def add_parts(parts, scale):
    return jnp.sum(parts.astype(F32), axis=0) * scale


def all_slices(piece):
    n = lax.axis_size("dp")
    copies = jnp.broadcast_to(piece[None], (n,) + piece.shape)
    return lax.all_to_all(copies, "dp", split_axis=0, concat_axis=0, tiled=True)


def sum_over_mp(value):
    n = lax.axis_size("mp")
    core = lax.axis_index("mp") % 2
    half = value.shape[0] // 2
    halves = value.reshape(2, half, value.shape[1])
    mine = lax.dynamic_index_in_dim(halves, core, 0, keepdims=False)
    other = lax.dynamic_index_in_dim(halves, 1 - core, 0, keepdims=False)
    swap = [(i, i ^ 1) for i in range(n)]
    mine = mine + lax.ppermute(other, "mp", swap)
    total = mine
    for d in range(2, n, 2):
        total = total + lax.ppermute(mine, "mp", [(i, i ^ d) for i in range(n)])
    other = lax.ppermute(total, "mp", swap)
    return jnp.where(core == 0, jnp.concatenate([total, other]), jnp.concatenate([other, total]))


def params():
    return pltpu.CompilerParams(vmem_limit_bytes=VMEM_BYTES)


def expand(x, weight, parts, me):
    blocks, hidden, feats = weight.shape
    tokens = x.shape[0]
    lanes = tokens // 128
    rows = hidden // parts * blocks

    def body(me_ref, x_ref, w_ref, *refs):
        outs, wide_ref = refs[:parts], refs[parts]
        for b in range(blocks):
            part = dot(w_ref[b], x_ref[:, b * feats : (b + 1) * feats], 1, 1)
            for c in range(lanes):
                wide_ref[c, pl.ds(b, hidden, stride=blocks), :] = part[:, c * 128 : (c + 1) * 128]
        for d in range(parts):
            start = pl.multiple_of((me_ref[0] ^ d) * rows, rows)
            for c in range(lanes):
                outs[d][:, c * 128 : (c + 1) * 128] = wide_ref[c, pl.ds(start, rows), :].astype(BF)

    return pl.pallas_call(
        body,
        in_specs=[pl.BlockSpec(memory_space=pltpu.SMEM)] + [pl.BlockSpec(memory_space=pltpu.VMEM)] * 2,
        out_specs=[pl.BlockSpec(memory_space=pltpu.VMEM)] * parts,
        out_shape=[jax.ShapeDtypeStruct((rows, tokens), BF)] * parts,
        scratch_shapes=[pltpu.VMEM((lanes, hidden * blocks, 128), F32)],
        compiler_params=params(),
        name="expand",
    )(me, x, weight)


def send(pieces, *which):
    n = len(pieces)
    return {d: lax.ppermute(pieces[d], "mp", [(i, i ^ d) for i in range(n)]) for d in which}


def together(*values):
    return lax.optimization_barrier(values)


def in_order(pieces, *groups):
    got = {0: pieces[0]}
    for group in groups:
        got.update(group)
    return [got[d] for d in range(len(pieces))]


STEP = 8


def gather_pair(refs, pair, me_ref, mix_ref):
    for d, ref in enumerate(refs):
        wide = ref[pair * 16 : pair * 16 + 16, :].astype(F32)
        at = pl.multiple_of((me_ref[0] ^ d) * 8, 8)
        for h in range(2):
            mix_ref[h, pl.ds(at, 8), :] = wide[h * 8 : h * 8 + 8]
    return [mix_ref[h].astype(BF) for h in range(2)]


def spread_pair(values, refs, pair, me_ref, mix_ref):
    for h in range(2):
        mix_ref[h] = values[h]
    for d, ref in enumerate(refs):
        at = pl.multiple_of((me_ref[0] ^ d) * 8, 8)
        block = jnp.concatenate([mix_ref[h, pl.ds(at, 8), :] for h in range(2)], axis=0)
        ref[pair * 16 : pair * 16 + 16, :] = block.astype(BF)


def middle_main(act, back, left_one, left_one_t, left_two_t, me):
    n = len(act)
    tokens = act[0].shape[1]
    units, width, _ = left_one.shape

    def body(me_ref, *refs):
        acts, backs, (one_ref, one_t_ref, two_t_ref) = refs[:n], refs[n : 2 * n], refs[2 * n : 2 * n + 3]
        outs = refs[2 * n + 3 : 3 * n + 3]
        x_ref, c_ref, hid_ref, bp_ref, mix_a, mix_c, mix_o = refs[3 * n + 3 :]
        for pair in range(STEP // 2):
            xs = gather_pair(acts, pair, me_ref, mix_a)
            cs = gather_pair(backs, pair, me_ref, mix_c)
            values = []
            for h in range(2):
                i = pair * 2 + h
                pre = dot(one_ref[i], xs[h], 1, 0)
                back_h = dot(two_t_ref[i], cs[h], 1, 0)
                cdf = 0.5 * (1.0 + lax.erf(pre * (1.0 / math.sqrt(2.0))))
                slope = cdf + pre * jnp.exp(-0.5 * pre * pre) * (1.0 / math.sqrt(2.0 * math.pi))
                back_pre = (back_h * slope).astype(BF)
                x_ref[i] = xs[h]
                c_ref[i] = cs[h]
                hid_ref[i] = (pre * cdf).astype(BF)
                bp_ref[i] = back_pre
                values.append(dot(one_t_ref[i], back_pre, 1, 0))
            spread_pair(values, outs, pair, me_ref, mix_o)

    piece = pl.BlockSpec((STEP * 8, tokens), lambda g: (g, 0))
    weights = pl.BlockSpec((STEP, width, width), lambda g: (g, 0, 0))
    local = pl.BlockSpec((STEP, width, tokens), lambda g: (g, 0, 0))
    results = pl.pallas_call(
        body,
        grid=(units // STEP,),
        in_specs=[pl.BlockSpec(memory_space=pltpu.SMEM)] + [piece] * (2 * n) + [weights] * 3,
        out_specs=[piece] * n + [local] * 4,
        out_shape=[jax.ShapeDtypeStruct(act[0].shape, BF)] * n
        + [jax.ShapeDtypeStruct((units, width, tokens), BF)] * 4,
        scratch_shapes=[pltpu.VMEM((2, width, tokens), F32)] * 3,
        compiler_params=params(),
        name="middle_main",
    )(me, *act, *back, left_one, left_one_t, left_two_t)
    return results[:n], results[n:]


def middle_rest(x, back, hid, back_pre, left_two, n, me):
    units, width, tokens = x.shape

    def body(me_ref, x_ref, c_ref, hid_ref, bp_ref, two_ref, *refs):
        outs, grad_ref, mix_o = refs[:n], refs[n], refs[n + 1]
        for pair in range(STEP // 2):
            values = []
            for h in range(2):
                i = pair * 2 + h
                values.append(dot(two_ref[i], hid_ref[i], 1, 0))
                grads = [dot(bp_ref[i], x_ref[i], 1, 1), dot(c_ref[i], hid_ref[i], 1, 1)]
                grad_ref[i] = jnp.concatenate(grads, axis=1).astype(BF)
            spread_pair(values, outs, pair, me_ref, mix_o)

    piece = pl.BlockSpec((STEP * 8, tokens), lambda g: (g, 0))
    weights = pl.BlockSpec((STEP, width, width), lambda g: (g, 0, 0))
    local = pl.BlockSpec((STEP, width, tokens), lambda g: (g, 0, 0))
    results = pl.pallas_call(
        body,
        grid=(units // STEP,),
        in_specs=[pl.BlockSpec(memory_space=pltpu.SMEM)] + [local] * 4 + [weights],
        out_specs=[piece] * n + [pl.BlockSpec((STEP, width, 2 * width), lambda g: (g, 0, 0))],
        out_shape=[jax.ShapeDtypeStruct((units * 8, tokens), BF)] * n
        + [jax.ShapeDtypeStruct((units, width, 2 * width), BF)],
        scratch_shapes=[pltpu.VMEM((2, width, tokens), F32)],
        compiler_params=params(),
        name="middle_rest",
    )(me, x, back, hid, back_pre, left_two)
    return results[:n], results[n]


def load_wide(pieces, me_ref, wide_ref):
    rows = pieces[0].shape[0]

    @pl.when(pl.program_id(0) == 0)
    def _():
        for d, ref in enumerate(pieces):
            start = pl.multiple_of((me_ref[0] ^ d) * rows, rows)
            for c in range(wide_ref.shape[0]):
                wide_ref[c, pl.ds(start, rows), :] = ref[:, c * 128 : (c + 1) * 128].astype(F32)


def pick_block(wide_ref, hidden, blocks):
    rows = pl.ds(pl.program_id(0), hidden, stride=blocks)
    parts = [wide_ref[c, rows, :].astype(BF) for c in range(wide_ref.shape[0])]
    return jnp.concatenate(parts, axis=1)


def output_side(act, zed, cot, right_two, me):
    n = len(act)
    rows, tokens = act[0].shape
    blocks, feats, hidden = right_two.shape

    def body(me_ref, *refs):
        z_ref, g_ref, w_ref, out_ref, r2_ref, wide_ref = refs[n:]
        load_wide(refs[:n], me_ref, wide_ref)
        mine = pick_block(wide_ref, hidden, blocks)
        last = dot(w_ref[0], mine, 1, 0)
        out_ref[...] = (z_ref[...].astype(F32) + last.T).astype(BF)
        r2_ref[0] = dot(g_ref[...], mine, 0, 1).astype(BF)

    column = pl.BlockSpec((tokens, feats), lambda b: (0, b))
    return pl.pallas_call(
        body,
        grid=(blocks,),
        in_specs=[pl.BlockSpec(memory_space=pltpu.SMEM)]
        + [pl.BlockSpec((rows, tokens), lambda b: (0, 0))] * n
        + [
            column,
            column,
            pl.BlockSpec((1, feats, hidden), lambda b: (b, 0, 0)),
        ],
        out_specs=[column, pl.BlockSpec((1, feats, hidden), lambda b: (b, 0, 0))],
        out_shape=[
            jax.ShapeDtypeStruct(zed.shape, BF),
            jax.ShapeDtypeStruct(right_two.shape, BF),
        ],
        scratch_shapes=[pltpu.VMEM((tokens // 128, n * rows, 128), F32)],
        compiler_params=params(),
        name="output_side",
    )(me, *act, zed, cot, right_two)


def by_residue(value, shape):
    parts, rows, cols = shape
    value = value.reshape(rows // 8, parts, 8, cols)
    moved = [value[:, p].reshape(rows, cols)[None] for p in range(parts)]
    return jnp.concatenate(moved, axis=0).astype(BF)


def input_side(act, zed, cot, mixed, gain, right_one_t, n_dp, me):
    n = len(act)
    rows, tokens = act[0].shape
    blocks, feats, hidden = right_one_t.shape

    def body(me_ref, *refs):
        z_ref, g_ref, m_ref, s_ref, w_ref, bz_ref, bm_ref, r1_ref, wide_ref = refs[n:]
        load_wide(refs[:n], me_ref, wide_ref)
        mine = pick_block(wide_ref, hidden, blocks)
        back_z = g_ref[...].astype(F32) + dot(w_ref[0], mine, 1, 0).T
        bz_ref[...] = back_z
        bm_ref[...] = by_residue(back_z * s_ref[...], bm_ref.shape)
        gain_part = jnp.sum(back_z * m_ref[...].astype(F32), axis=0, keepdims=True)
        high = gain_part.astype(BF).astype(F32)
        row = lax.broadcasted_iota(jnp.int32, (8, feats), 0)
        tail = jnp.where(row == 0, high, jnp.where(row == 1, gain_part - high, 0.0)).astype(BF)
        grad = dot(mine, z_ref[...], 1, 0).astype(BF)
        for h in range(2):
            r1_ref[h, : hidden // 2, :] = grad[h * hidden // 2 : (h + 1) * hidden // 2]
            r1_ref[h, hidden // 2 :, :] = tail

    column = pl.BlockSpec((tokens, feats), lambda b: (0, b))
    row = pl.BlockSpec((1, feats), lambda b: (0, b))
    return pl.pallas_call(
        body,
        grid=(blocks,),
        in_specs=[pl.BlockSpec(memory_space=pltpu.SMEM)]
        + [pl.BlockSpec((rows, tokens), lambda b: (0, 0))] * n
        + [
            column,
            column,
            column,
            row,
            pl.BlockSpec((1, feats, hidden), lambda b: (b, 0, 0)),
        ],
        out_specs=[
            column,
            pl.BlockSpec((n_dp, tokens // n_dp, feats), lambda b: (0, 0, b)),
            pl.BlockSpec((2, hidden // 2 + 8, feats), lambda b: (b, 0, 0)),
        ],
        out_shape=[
            jax.ShapeDtypeStruct(zed.shape, F32),
            jax.ShapeDtypeStruct((n_dp, tokens // n_dp, zed.shape[1]), BF),
            jax.ShapeDtypeStruct((blocks * 2, hidden // 2 + 8, feats), BF),
        ],
        scratch_shapes=[pltpu.VMEM((tokens // 128, n * rows, 128), F32)],
        compiler_params=params(),
        name="input_side",
    )(me, *act, zed, cot, mixed, gain, right_one_t)


def per_device(
    tokens, cotangent, seq_right, seq_left, seq_gain, right_one, left_one, left_two, right_two
):
    rows_here, cols_here = tokens.shape
    block_len = seq_right.shape[1]
    blocks_here = rows_here // block_len
    n_mp = lax.axis_size("mp")
    me = lax.axis_index("mp").astype(jnp.int32)
    me1 = me.reshape(1)
    scale_rows = float(rows_here * lax.axis_size("dp")) ** (-0.5)
    scale_cols = float(cols_here * n_mp) ** (-0.5)

    pieces = expand(cotangent, jnp.swapaxes(right_two, 1, 2), n_mp, me1)
    seq_view = tokens.reshape(blocks_here, block_len, cols_here)
    first = product("sij,sjc->sic", seq_right, seq_view).astype(BF)
    first, pieces = together(first, pieces)
    back_c1 = send(pieces, 2, 6, 1, 3, 7)
    first_moved = lax.all_to_all(first, "dp", split_axis=1, concat_axis=0, tiled=True)
    first_moved, back_c1 = together(first_moved, back_c1)
    mixed_moved = product("isk,kic->sic", seq_left, first_moved).astype(BF)
    back_c2 = send(pieces, 4, 5)
    mixed = lax.all_to_all(mixed_moved, "dp", split_axis=0, concat_axis=1, tiled=True)
    mixed = mixed.reshape(rows_here, cols_here)
    mixed, back_c2 = together(mixed, back_c2)
    back_c = in_order(pieces, back_c1, back_c2)
    zed = (tokens.astype(F32) + seq_gain * mixed.astype(F32)).astype(BF)

    pieces = expand(zed, right_one, n_mp, me1)
    act_a = in_order(pieces, send(pieces, 2, 6, 4, 3, 7, 5, 1))
    pieces, (x, back, hid, back_pre) = middle_main(
        act_a, back_c, left_one, jnp.swapaxes(left_one, 1, 2), jnp.swapaxes(left_two, 1, 2), me1
    )
    back_a1 = send(pieces, 2, 6, 3, 7, 1)
    pieces_c, part_left = middle_rest(x, back, hid, back_pre, left_two, n_mp, me1)
    right_one_t = jnp.swapaxes(right_one, 1, 2)
    part_left, back_a1, right_one_t = together(part_left, back_a1, right_one_t)
    back_a2 = send(pieces, 4, 5)
    back_a = in_order(pieces, back_a1, back_a2)
    left_parts = slice_parts(part_left)

    pieces_c, back_a = together(pieces_c, back_a)
    act_c1 = send(pieces_c, 2, 6)
    back_z, back_mixed, part_r1 = input_side(
        back_a,
        zed,
        cotangent,
        mixed,
        seq_gain.reshape(1, cols_here),
        right_one_t,
        lax.axis_size("dp"),
        me1,
    )
    back_mixed, act_c1, left_parts = together(back_mixed, act_c1, left_parts)
    back_z = back_z.reshape(blocks_here, block_len, cols_here)
    act_c2 = send(pieces_c, 3, 7, 1)
    back_mixed_moved = lax.all_to_all(back_mixed, "dp", split_axis=0, concat_axis=0, tiled=True)
    back_mixed_moved = back_mixed_moved.reshape(first_moved.shape)
    back_mixed_moved, act_c2, part_r1 = together(back_mixed_moved, act_c2, part_r1)
    back_first_moved = product("isk,sic->kic", seq_left, back_mixed_moved).astype(BF)
    part_seq_left = product("sic,kic->isk", back_mixed_moved, first_moved)
    act_c3 = send(pieces_c, 4, 5)
    r1_parts = slice_parts(part_r1)
    back_first_moved, r1_parts, act_c3 = together(back_first_moved, r1_parts, act_c3)
    back_first = lax.all_to_all(back_first_moved, "dp", split_axis=0, concat_axis=1, tiled=True)
    act_c = in_order(pieces_c, act_c1, act_c2, act_c3)
    slice_left = add_parts(left_parts, scale_rows)
    slice_r1 = add_parts(r1_parts, scale_rows)
    half = right_one.shape[1] // 2
    slice_gain = slice_r1[half : half + 1] + slice_r1[half + 1 : half + 2]
    slice_gain = jnp.broadcast_to(slice_gain, (8, block_len))
    slices = jnp.concatenate([slice_left, slice_r1[:half], slice_gain]).astype(BF)
    rows_left = slice_left.shape[0]
    gathered = lax.all_gather(slices, "dp")

    output, part_r2 = output_side(act_c, zed, cotangent, right_two, me1)
    back_first, part_r2 = together(back_first, part_r2)
    slice_r2 = add_parts(slice_parts(part_r2), scale_rows).astype(BF)
    sum_r2 = all_slices(slice_r2)
    gathered = gathered.astype(F32)
    sum_left = gathered[:, :rows_left].reshape(part_left.shape)
    sum_r1 = gathered[:, rows_left : rows_left + half].reshape(right_one.shape)
    sum_gain = gathered[::2, rows_left + half].reshape(cols_here)
    sum_r2 = sum_r2.astype(F32)

    grad_tokens = (back_z + product("sij,sic->sjc", seq_right, back_first)).astype(BF)
    part_seq_right = product("sic,sjc->sij", back_first, seq_view)
    seq_sum = sum_over_mp(
        jnp.concatenate([part_seq_right.reshape(-1, 128), part_seq_left.reshape(-1, 128)])
    )
    seq_rows = part_seq_right.size // 128
    return (
        output,
        grad_tokens.reshape(rows_here, cols_here),
        seq_sum[:seq_rows].reshape(part_seq_right.shape) * scale_cols,
        seq_sum[seq_rows:].reshape(part_seq_left.shape) * scale_cols,
        sum_gain,
        sum_r1,
        sum_left[:, :, : left_one.shape[2]],
        sum_left[:, :, left_one.shape[2] :],
        sum_r2.reshape(right_two.shape),
    )


def solution(mesh):
    specs = (
        P("dp", "mp"),
        P("dp", "mp"),
        P("dp", None, None),
        P("dp", None, None),
        P("mp"),
        P("mp", None, None),
        P("mp", None, None),
        P("mp", None, None),
        P("mp", None, None),
    )
    return jax.shard_map(per_device, mesh=mesh, in_specs=specs, out_specs=specs, check_vma=False)
```

```python
import math

import jax
import jax.numpy as jnp
from jax import lax
from jax.experimental import pallas as pl
from jax.experimental.pallas import tpu as pltpu
from jax.sharding import PartitionSpec as P

BF = jnp.bfloat16
F32 = jnp.float32
VMEM_BYTES = 56 * 1024 * 1024


def dot(left_arg, right_arg, left_dim, right_dim):
    return lax.dot_general(
        left_arg,
        right_arg,
        (((left_dim,), (right_dim,)), ((), ())),
        preferred_element_type=F32,
    )


def product(form, left_arg, right_arg):
    return jnp.einsum(form, left_arg, right_arg, preferred_element_type=F32)


def slice_parts(parts):
    n = lax.axis_size("dp")
    parts = parts.reshape(n, -1, parts.shape[-1])
    return lax.all_to_all(parts, "dp", split_axis=0, concat_axis=0, tiled=True)


def add_parts(parts, scale):
    return jnp.sum(parts.astype(F32), axis=0) * scale


def all_slices(piece):
    n = lax.axis_size("dp")
    copies = jnp.broadcast_to(piece[None], (n,) + piece.shape)
    return lax.all_to_all(copies, "dp", split_axis=0, concat_axis=0, tiled=True)


def sum_over_mp(value):
    n = lax.axis_size("mp")
    core = lax.axis_index("mp") % 2
    half = value.shape[0] // 2
    halves = value.reshape(2, half, value.shape[1])
    mine = lax.dynamic_index_in_dim(halves, core, 0, keepdims=False)
    other = lax.dynamic_index_in_dim(halves, 1 - core, 0, keepdims=False)
    swap = [(i, i ^ 1) for i in range(n)]
    mine = mine + lax.ppermute(other, "mp", swap)
    total = mine
    for d in range(2, n, 2):
        total = total + lax.ppermute(mine, "mp", [(i, i ^ d) for i in range(n)])
    other = lax.ppermute(total, "mp", swap)
    return jnp.where(core == 0, jnp.concatenate([total, other]), jnp.concatenate([other, total]))


def params():
    return pltpu.CompilerParams(vmem_limit_bytes=VMEM_BYTES)


def expand(x, weight, parts, me):
    blocks, hidden, feats = weight.shape
    tokens = x.shape[0]
    lanes = tokens // 128
    rows = hidden // parts * blocks

    def body(me_ref, x_ref, w_ref, *refs):
        outs, wide_ref = refs[:parts], refs[parts]
        for b in range(blocks):
            part = dot(w_ref[b], x_ref[:, b * feats : (b + 1) * feats], 1, 1)
            for c in range(lanes):
                wide_ref[c, pl.ds(b, hidden, stride=blocks), :] = part[:, c * 128 : (c + 1) * 128]
        for d in range(parts):
            start = pl.multiple_of((me_ref[0] ^ d) * rows, rows)
            for c in range(lanes):
                outs[d][:, c * 128 : (c + 1) * 128] = wide_ref[c, pl.ds(start, rows), :].astype(BF)

    return pl.pallas_call(
        body,
        in_specs=[pl.BlockSpec(memory_space=pltpu.SMEM)] + [pl.BlockSpec(memory_space=pltpu.VMEM)] * 2,
        out_specs=[pl.BlockSpec(memory_space=pltpu.VMEM)] * parts,
        out_shape=[jax.ShapeDtypeStruct((rows, tokens), BF)] * parts,
        scratch_shapes=[pltpu.VMEM((lanes, hidden * blocks, 128), F32)],
        compiler_params=params(),
        name="expand",
    )(me, x, weight)


def send(pieces, *which):
    n = len(pieces)
    return {d: lax.ppermute(pieces[d], "mp", [(i, i ^ d) for i in range(n)]) for d in which}


def together(*values):
    return lax.optimization_barrier(values)


def in_order(pieces, *groups):
    got = {0: pieces[0]}
    for group in groups:
        got.update(group)
    return [got[d] for d in range(len(pieces))]


STEP = 8


def gather_pair(refs, pair, me_ref, mix_ref):
    for d, ref in enumerate(refs):
        wide = ref[pair * 16 : pair * 16 + 16, :].astype(F32)
        at = pl.multiple_of((me_ref[0] ^ d) * 8, 8)
        for h in range(2):
            mix_ref[h, pl.ds(at, 8), :] = wide[h * 8 : h * 8 + 8]
    return [mix_ref[h].astype(BF) for h in range(2)]


def spread_pair(values, refs, pair, me_ref, mix_ref):
    for h in range(2):
        mix_ref[h] = values[h]
    for d, ref in enumerate(refs):
        at = pl.multiple_of((me_ref[0] ^ d) * 8, 8)
        block = jnp.concatenate([mix_ref[h, pl.ds(at, 8), :] for h in range(2)], axis=0)
        ref[pair * 16 : pair * 16 + 16, :] = block.astype(BF)


def middle_main(act, back, left_one, left_one_t, left_two_t, me):
    n = len(act)
    tokens = act[0].shape[1]
    units, width, _ = left_one.shape

    def body(me_ref, *refs):
        acts, backs, (one_ref, one_t_ref, two_t_ref) = refs[:n], refs[n : 2 * n], refs[2 * n : 2 * n + 3]
        outs = refs[2 * n + 3 : 3 * n + 3]
        x_ref, c_ref, hid_ref, bp_ref, mix_a, mix_c, mix_o = refs[3 * n + 3 :]
        for pair in range(STEP // 2):
            xs = gather_pair(acts, pair, me_ref, mix_a)
            cs = gather_pair(backs, pair, me_ref, mix_c)
            values = []
            for h in range(2):
                i = pair * 2 + h
                pre = dot(one_ref[i], xs[h], 1, 0)
                back_h = dot(two_t_ref[i], cs[h], 1, 0)
                cdf = 0.5 * (1.0 + lax.erf(pre * (1.0 / math.sqrt(2.0))))
                slope = cdf + pre * jnp.exp(-0.5 * pre * pre) * (1.0 / math.sqrt(2.0 * math.pi))
                back_pre = (back_h * slope).astype(BF)
                x_ref[i] = xs[h]
                c_ref[i] = cs[h]
                hid_ref[i] = (pre * cdf).astype(BF)
                bp_ref[i] = back_pre
                values.append(dot(one_t_ref[i], back_pre, 1, 0))
            spread_pair(values, outs, pair, me_ref, mix_o)

    piece = pl.BlockSpec((STEP * 8, tokens), lambda g: (g, 0))
    weights = pl.BlockSpec((STEP, width, width), lambda g: (g, 0, 0))
    local = pl.BlockSpec((STEP, width, tokens), lambda g: (g, 0, 0))
    results = pl.pallas_call(
        body,
        grid=(units // STEP,),
        in_specs=[pl.BlockSpec(memory_space=pltpu.SMEM)] + [piece] * (2 * n) + [weights] * 3,
        out_specs=[piece] * n + [local] * 4,
        out_shape=[jax.ShapeDtypeStruct(act[0].shape, BF)] * n
        + [jax.ShapeDtypeStruct((units, width, tokens), BF)] * 4,
        scratch_shapes=[pltpu.VMEM((2, width, tokens), F32)] * 3,
        compiler_params=params(),
        name="middle_main",
    )(me, *act, *back, left_one, left_one_t, left_two_t)
    return results[:n], results[n:]


def middle_rest(x, back, hid, back_pre, left_two, n, me):
    units, width, tokens = x.shape

    def body(me_ref, x_ref, c_ref, hid_ref, bp_ref, two_ref, *refs):
        outs, grad_ref, mix_o = refs[:n], refs[n], refs[n + 1]
        for pair in range(STEP // 2):
            values = []
            for h in range(2):
                i = pair * 2 + h
                values.append(dot(two_ref[i], hid_ref[i], 1, 0))
                grads = [dot(bp_ref[i], x_ref[i], 1, 1), dot(c_ref[i], hid_ref[i], 1, 1)]
                grad_ref[i] = jnp.concatenate(grads, axis=1).astype(BF)
            spread_pair(values, outs, pair, me_ref, mix_o)

    piece = pl.BlockSpec((STEP * 8, tokens), lambda g: (g, 0))
    weights = pl.BlockSpec((STEP, width, width), lambda g: (g, 0, 0))
    local = pl.BlockSpec((STEP, width, tokens), lambda g: (g, 0, 0))
    results = pl.pallas_call(
        body,
        grid=(units // STEP,),
        in_specs=[pl.BlockSpec(memory_space=pltpu.SMEM)] + [local] * 4 + [weights],
        out_specs=[piece] * n + [pl.BlockSpec((STEP, width, 2 * width), lambda g: (g, 0, 0))],
        out_shape=[jax.ShapeDtypeStruct((units * 8, tokens), BF)] * n
        + [jax.ShapeDtypeStruct((units, width, 2 * width), BF)],
        scratch_shapes=[pltpu.VMEM((2, width, tokens), F32)],
        compiler_params=params(),
        name="middle_rest",
    )(me, x, back, hid, back_pre, left_two)
    return results[:n], results[n]


def load_wide(pieces, me_ref, wide_ref):
    rows = pieces[0].shape[0]

    @pl.when(pl.program_id(0) == 0)
    def _():
        for d, ref in enumerate(pieces):
            start = pl.multiple_of((me_ref[0] ^ d) * rows, rows)
            for c in range(wide_ref.shape[0]):
                wide_ref[c, pl.ds(start, rows), :] = ref[:, c * 128 : (c + 1) * 128].astype(F32)


def pick_block(wide_ref, hidden, blocks):
    rows = pl.ds(pl.program_id(0), hidden, stride=blocks)
    parts = [wide_ref[c, rows, :].astype(BF) for c in range(wide_ref.shape[0])]
    return jnp.concatenate(parts, axis=1)


def output_side(act, zed, cot, right_two, me):
    n = len(act)
    rows, tokens = act[0].shape
    blocks, feats, hidden = right_two.shape

    def body(me_ref, *refs):
        z_ref, g_ref, w_ref, out_ref, r2_ref, wide_ref = refs[n:]
        load_wide(refs[:n], me_ref, wide_ref)
        mine = pick_block(wide_ref, hidden, blocks)
        last = dot(w_ref[0], mine, 1, 0)
        out_ref[...] = (z_ref[...].astype(F32) + last.T).astype(BF)
        r2_ref[0] = dot(g_ref[...], mine, 0, 1).astype(BF)

    column = pl.BlockSpec((tokens, feats), lambda b: (0, b))
    return pl.pallas_call(
        body,
        grid=(blocks,),
        in_specs=[pl.BlockSpec(memory_space=pltpu.SMEM)]
        + [pl.BlockSpec((rows, tokens), lambda b: (0, 0))] * n
        + [
            column,
            column,
            pl.BlockSpec((1, feats, hidden), lambda b: (b, 0, 0)),
        ],
        out_specs=[column, pl.BlockSpec((1, feats, hidden), lambda b: (b, 0, 0))],
        out_shape=[
            jax.ShapeDtypeStruct(zed.shape, BF),
            jax.ShapeDtypeStruct(right_two.shape, BF),
        ],
        scratch_shapes=[pltpu.VMEM((tokens // 128, n * rows, 128), F32)],
        compiler_params=params(),
        name="output_side",
    )(me, *act, zed, cot, right_two)


def by_residue(value, shape):
    parts, rows, cols = shape
    value = value.reshape(rows // 8, parts, 8, cols)
    moved = [value[:, p].reshape(rows, cols)[None] for p in range(parts)]
    return jnp.concatenate(moved, axis=0).astype(BF)


def input_side(act, zed, cot, mixed, gain, right_one_t, n_dp, me):
    n = len(act)
    rows, tokens = act[0].shape
    blocks, feats, hidden = right_one_t.shape

    def body(me_ref, *refs):
        z_ref, g_ref, m_ref, s_ref, w_ref, bz_ref, bm_ref, r1_ref, wide_ref = refs[n:]
        load_wide(refs[:n], me_ref, wide_ref)
        mine = pick_block(wide_ref, hidden, blocks)
        back_z = g_ref[...].astype(F32) + dot(w_ref[0], mine, 1, 0).T
        bz_ref[...] = back_z
        bm_ref[...] = by_residue(back_z * s_ref[...], bm_ref.shape)
        gain_part = jnp.sum(back_z * m_ref[...].astype(F32), axis=0, keepdims=True)
        high = gain_part.astype(BF).astype(F32)
        row = lax.broadcasted_iota(jnp.int32, (8, feats), 0)
        tail = jnp.where(row == 0, high, jnp.where(row == 1, gain_part - high, 0.0)).astype(BF)
        grad = dot(mine, z_ref[...], 1, 0).astype(BF)
        for h in range(2):
            r1_ref[h, : hidden // 2, :] = grad[h * hidden // 2 : (h + 1) * hidden // 2]
            r1_ref[h, hidden // 2 :, :] = tail

    column = pl.BlockSpec((tokens, feats), lambda b: (0, b))
    row = pl.BlockSpec((1, feats), lambda b: (0, b))
    return pl.pallas_call(
        body,
        grid=(blocks,),
        in_specs=[pl.BlockSpec(memory_space=pltpu.SMEM)]
        + [pl.BlockSpec((rows, tokens), lambda b: (0, 0))] * n
        + [
            column,
            column,
            column,
            row,
            pl.BlockSpec((1, feats, hidden), lambda b: (b, 0, 0)),
        ],
        out_specs=[
            column,
            pl.BlockSpec((n_dp, tokens // n_dp, feats), lambda b: (0, 0, b)),
            pl.BlockSpec((2, hidden // 2 + 8, feats), lambda b: (b, 0, 0)),
        ],
        out_shape=[
            jax.ShapeDtypeStruct(zed.shape, F32),
            jax.ShapeDtypeStruct((n_dp, tokens // n_dp, zed.shape[1]), BF),
            jax.ShapeDtypeStruct((blocks * 2, hidden // 2 + 8, feats), BF),
        ],
        scratch_shapes=[pltpu.VMEM((tokens // 128, n * rows, 128), F32)],
        compiler_params=params(),
        name="input_side",
    )(me, *act, zed, cot, mixed, gain, right_one_t)


def per_device(
    tokens, cotangent, seq_right, seq_left, seq_gain, right_one, left_one, left_two, right_two
):
    rows_here, cols_here = tokens.shape
    block_len = seq_right.shape[1]
    blocks_here = rows_here // block_len
    n_mp = lax.axis_size("mp")
    me = lax.axis_index("mp").astype(jnp.int32)
    me1 = me.reshape(1)
    scale_rows = float(rows_here * lax.axis_size("dp")) ** (-0.5)
    scale_cols = float(cols_here * n_mp) ** (-0.5)

    pieces = expand(cotangent, jnp.swapaxes(right_two, 1, 2), n_mp, me1)
    seq_view = tokens.reshape(blocks_here, block_len, cols_here)
    first = product("sij,sjc->sic", seq_right, seq_view).astype(BF)
    first, pieces = together(first, pieces)
    back_c1 = send(pieces, 2, 6, 1, 3, 7)
    first_moved = lax.all_to_all(first, "dp", split_axis=1, concat_axis=0, tiled=True)
    first_moved, back_c1 = together(first_moved, back_c1)
    mixed_moved = product("isk,kic->sic", seq_left, first_moved).astype(BF)
    back_c2 = send(pieces, 4, 5)
    mixed = lax.all_to_all(mixed_moved, "dp", split_axis=0, concat_axis=1, tiled=True)
    mixed = mixed.reshape(rows_here, cols_here)
    mixed, back_c2 = together(mixed, back_c2)
    back_c = in_order(pieces, back_c1, back_c2)
    zed = (tokens.astype(F32) + seq_gain * mixed.astype(F32)).astype(BF)

    pieces = expand(zed, right_one, n_mp, me1)
    act_a = in_order(pieces, send(pieces, 2, 6, 4, 3, 7, 5, 1))
    pieces, (x, back, hid, back_pre) = middle_main(
        act_a, back_c, left_one, jnp.swapaxes(left_one, 1, 2), jnp.swapaxes(left_two, 1, 2), me1
    )
    back_a1 = send(pieces, 2, 6, 3, 7, 1)
    pieces_c, part_left = middle_rest(x, back, hid, back_pre, left_two, n_mp, me1)
    right_one_t = jnp.swapaxes(right_one, 1, 2)
    part_left, back_a1, right_one_t = together(part_left, back_a1, right_one_t)
    back_a2 = send(pieces, 4, 5)
    back_a = in_order(pieces, back_a1, back_a2)
    left_parts = slice_parts(part_left)

    pieces_c, back_a = together(pieces_c, back_a)
    act_c1 = send(pieces_c, 2, 6, 1)
    back_z, back_mixed, part_r1 = input_side(
        back_a,
        zed,
        cotangent,
        mixed,
        seq_gain.reshape(1, cols_here),
        right_one_t,
        lax.axis_size("dp"),
        me1,
    )
    back_mixed, act_c1, left_parts = together(back_mixed, act_c1, left_parts)
    back_z = back_z.reshape(blocks_here, block_len, cols_here)
    act_c2 = send(pieces_c, 3, 7)
    back_mixed_moved = lax.all_to_all(back_mixed, "dp", split_axis=0, concat_axis=0, tiled=True)
    back_mixed_moved = back_mixed_moved.reshape(first_moved.shape)
    back_mixed_moved, act_c2, part_r1 = together(back_mixed_moved, act_c2, part_r1)
    back_first_moved = product("isk,sic->kic", seq_left, back_mixed_moved).astype(BF)
    part_seq_left = product("sic,kic->isk", back_mixed_moved, first_moved)
    act_c3 = send(pieces_c, 4, 5)
    r1_parts = slice_parts(part_r1)
    back_first_moved, r1_parts, act_c3 = together(back_first_moved, r1_parts, act_c3)
    back_first = lax.all_to_all(back_first_moved, "dp", split_axis=0, concat_axis=1, tiled=True)
    act_c = in_order(pieces_c, act_c1, act_c2, act_c3)
    slice_left = add_parts(left_parts, scale_rows)
    slice_r1 = add_parts(r1_parts, scale_rows)
    half = right_one.shape[1] // 2
    slice_gain = slice_r1[half : half + 1] + slice_r1[half + 1 : half + 2]
    slice_gain = jnp.broadcast_to(slice_gain, (8, block_len))
    slices = jnp.concatenate([slice_left, slice_r1[:half], slice_gain]).astype(BF)
    rows_left = slice_left.shape[0]
    gathered = lax.all_gather(slices, "dp")

    output, part_r2 = output_side(act_c, zed, cotangent, right_two, me1)
    back_first, part_r2 = together(back_first, part_r2)
    slice_r2 = add_parts(slice_parts(part_r2), scale_rows).astype(BF)
    sum_r2 = all_slices(slice_r2)
    gathered = gathered.astype(F32)
    sum_left = gathered[:, :rows_left].reshape(part_left.shape)
    sum_r1 = gathered[:, rows_left : rows_left + half].reshape(right_one.shape)
    sum_gain = gathered[::2, rows_left + half].reshape(cols_here)
    sum_r2 = sum_r2.astype(F32)

    grad_tokens = (back_z + product("sij,sic->sjc", seq_right, back_first)).astype(BF)
    part_seq_right = product("sic,sjc->sij", back_first, seq_view)
    seq_sum = sum_over_mp(
        jnp.concatenate([part_seq_right.reshape(-1, 128), part_seq_left.reshape(-1, 128)])
    )
    seq_rows = part_seq_right.size // 128
    return (
        output,
        grad_tokens.reshape(rows_here, cols_here),
        seq_sum[:seq_rows].reshape(part_seq_right.shape) * scale_cols,
        seq_sum[seq_rows:].reshape(part_seq_left.shape) * scale_cols,
        sum_gain,
        sum_r1,
        sum_left[:, :, : left_one.shape[2]],
        sum_left[:, :, left_one.shape[2] :],
        sum_r2.reshape(right_two.shape),
    )


def solution(mesh):
    specs = (
        P("dp", "mp"),
        P("dp", "mp"),
        P("dp", None, None),
        P("dp", None, None),
        P("mp"),
        P("mp", None, None),
        P("mp", None, None),
        P("mp", None, None),
        P("mp", None, None),
    )
    return jax.shard_map(per_device, mesh=mesh, in_specs=specs, out_specs=specs, check_vma=False)
```
